32 devices in a mesh: grp: 2 (over y), row: 4 (over z), col: 2 (over x), sub: 2 (over core).
Axes of the slice: x: 2, y: 2, z: 4, core: 2. Of those that a mesh axis runs over, the one named last changes fastest.
Arguments:
- pair: bfloat16 [96, 48, 128], P(('grp', 'row'), 'col'), parts along dimension 0, may hold values from -6 to 6
- length: int32 [2], P('grp'), parts along dimension 0, may hold values from 24 to 48
- chain: int32 [96], P('grp'), parts along dimension 0, may hold values from 0 to 3, never falling along the last dimension, each value on 1 to 24 neighbouring positions
- att_proj: bfloat16 [128, 4, 128], P(None, None, 'sub'), may hold values from -0.5 to 0.5
- att_bias: bfloat16 [128, 4], P(None, 'sub')
- chain_bias: float32 [4], P('sub'), may hold values from -2 to 2
- att_out: bfloat16 [128, 128], P('sub'), may hold values from -0.5 to 0.5
- mult_in: bfloat16 [128, 512], replicated, may hold values from -0.5 to 0.5
- mult_gate: bfloat16 [128, 128], replicated, may hold values from -0.5 to 0.5
- mult_out: bfloat16 [128, 128], replicated, may hold values from -0.5 to 0.5
- trans_up: bfloat16 [128, 512], replicated, may hold values from -0.5 to 0.5
- trans_down: bfloat16 [512, 128], replicated, may hold values from -0.25 to 0.25
Outputs:
- pair_out: bfloat16 [96, 48, 128], P(('grp', 'row'), ('col', 'sub')), parts along dimension 0
The draws below stay inside these ranges and needn't reach their ends.
There are 2 independent parts, one for each index of `grp`. The reference program is written for one: setup_inputs(seed, part) draws one part's arguments, and reference() takes and returns one part's arrays. A program takes and returns all parts, laid end to end along the dimension named above; an argument that names none is the same for every part. Nothing has to cross between parts.
Inputs may be any that keep to these rules, and one draw needn't show every extreme that they name: chain numbers never fall along the residues; each chain has 1 to 24 residues.
All inputs are finite; a program needn't handle non-finite values.
Results may differ from the reference program's by a relative error of at most 0.012.
The reference program's roundings to bfloat16 on the way (of `normed`, `weights`, `attended`, `mixed` and `hidden`) count: a program that leaves them out, or rounds other values in their place, can miss the bound.
Values may be sent and summed in bfloat16 or wider, within the bound.
No kernel may reach another device: no remote copies, remote signals or barrier semaphores. Data moves between devices by JAX's collectives and lax.ppermute only.
A program may use at most 64 MiB of HBM per device.

```python
import math
import jax
import jax.numpy as jnp
import numpy as np
from jax import lax

PAIR = 128
HEADS = 4
HEAD_DIM = 32
MULT = 128
TRANS = 512
RES = 48
N_COL = 2
N_SUB = 2


def draw_att_bias(key, part):
    first_key = jax.random.fold_in(key, 11)
    weights = jnp.clip(jax.random.normal(first_key, (PAIR, HEADS), jnp.float32), -6.0, 6.0) * PAIR ** (-0.5)
    return weights.astype(jnp.bfloat16)


def levels(stream_key, dims, pieces, low, high):
    def one(dim, parts):
        steps = jax.random.uniform(jax.random.fold_in(jax.random.fold_in(stream_key, 6), dim), (parts,), jnp.float32, low / len(pieces), high / len(pieces))
        return jnp.repeat(jnp.exp(steps), dims[dim] // parts).reshape((-1,) + (1,) * (len(dims) - dim - 1))

    level = one(*pieces[0])
    for cut in pieces[1:]:
        level = level * one(*cut)
    return level


def split_up(number_of, total, limit, slope):
    portions = [(1 << 20) // math.isqrt(rank ** slope) + 1 for rank in range(2, number_of + 1)]
    surplus, given = total - limit - (number_of - 1), [1] * (number_of - 1)
    while surplus > 0:
        movable = [i for i in range(number_of - 1) if given[i] < limit]
        mass, remaining = sum([portions[i] for i in movable]), surplus
        for i in movable:
            addition = min(limit - given[i], max(1, remaining * portions[i] // mass), surplus)
            given[i] = given[i] + addition
            surplus = surplus - addition
    return np.array([limit] + given)


def uneven(rng, amount, total, limit, lean):
    if amount == 2:
        one = jax.random.randint(rng, (), max(1, total - limit), min(limit, total - 1) + 1)
        return jnp.stack([one, total - one])
    lengths = jnp.asarray(split_up(amount, total, limit, lean), jnp.int32)
    couples = (amount - 1) // 2
    source_of, receiver = lengths[1:1 + 2 * couples:2], lengths[2:2 + 2 * couples:2]
    margin = jnp.minimum(source_of - 1, limit - receiver)
    moved = jax.random.randint(jax.random.fold_in(rng, 1), (couples,), 0, 1 << 20) % (margin + 1)
    lengths = lengths.at[1:1 + 2 * couples:2].set(source_of - moved).at[2:2 + 2 * couples:2].set(receiver + moved)
    return lengths[jax.random.permutation(jax.random.fold_in(rng, 2), amount)]


def bell_draw(own_key, extent, scale, limit, shards=(), held_as=jnp.bfloat16):
    loudness = levels(own_key, extent, shards, -0.22, 0.18) if shards else 1.0
    drawn = jax.random.normal(own_key, extent, jnp.float32) * scale * loudness
    return jnp.minimum(jnp.maximum(drawn, -limit), limit).astype(held_as)


def setup_inputs(seed: int = 0, part: int = 0) -> dict:
    key_list = jax.random.split(jax.random.key(seed), 13)
    part_splits = jax.random.split(jax.random.fold_in(key_list[12], part), 13)
    return {
        "pair": bell_draw(part_splits[0], (RES, RES, PAIR), 1.0, 6.0, ((0, 4), (1, 2))),
        "length": jax.random.randint(part_splits[1], (1,), RES // 2, RES + 1).astype(jnp.int32),
        "chain": jnp.searchsorted(jnp.cumsum(uneven(part_splits[2], 4, RES, RES // 2, 1)), jnp.arange(RES), side="right").astype(jnp.int32),
        "att_proj": bell_draw(key_list[3], (PAIR, 4, HEADS * HEAD_DIM), PAIR ** -0.5, 0.5, ((2, 2),)),
        "att_bias": draw_att_bias(jax.random.fold_in(key_list[12], 71), part),
        "chain_bias": jnp.clip(jax.random.uniform(key_list[5], (HEADS,), jnp.float32, -2.0, 2.0) * levels(key_list[5], (HEADS,), ((0, 2),), -0.4, 0.0), -2.0, 2.0),
        "att_out": bell_draw(key_list[6], (HEADS * HEAD_DIM, PAIR), (HEADS * HEAD_DIM) ** -0.5, 0.5, ((0, 2),)),
        "mult_in": bell_draw(key_list[7], (PAIR, 4 * MULT), PAIR ** -0.5, 0.5),
        "mult_gate": bell_draw(key_list[8], (PAIR, PAIR), PAIR ** -0.5, 0.5),
        "mult_out": bell_draw(key_list[9], (MULT, PAIR), MULT ** -0.5, 0.5),
        "trans_up": bell_draw(key_list[10], (PAIR, TRANS), PAIR ** -0.5, 0.5),
        "trans_down": bell_draw(key_list[11], (TRANS, PAIR), TRANS ** -0.5, 0.25),
    }


def norm(value):
    mean = lax.optimization_barrier(jnp.mean(value, axis=-1, keepdims=True))
    centred = value - mean
    variance = lax.optimization_barrier(jnp.mean(centred * centred, axis=-1, keepdims=True))
    return centred * lax.rsqrt(variance + 1e-05)

def reference(pair, length, chain, att_proj, att_bias, chain_bias, att_out, mult_in, mult_gate, mult_out, trans_up, trans_down):
    width = PAIR
    spread = HEADS * HEAD_DIM
    valid = (jnp.arange(RES) < length[0]).astype(jnp.float32)
    normed = norm(pair.astype(jnp.float32)).astype(jnp.bfloat16)
    flat = normed.reshape(RES * RES, width)
    projected = jnp.dot(flat, att_proj.reshape(width, 4 * spread), preferred_element_type=jnp.float32).reshape(RES, RES, 4, spread)
    query = (projected[:, :, 0] * HEAD_DIM ** (-0.5)).astype(jnp.bfloat16).reshape(RES // 2, 2, RES, HEADS, HEAD_DIM)
    keys = projected[:, :, 1].astype(jnp.bfloat16).reshape(RES // 2, 2, RES, HEADS, HEAD_DIM)
    values = projected[:, :, 2].astype(jnp.bfloat16).reshape(RES // 2, 2, RES, HEADS, HEAD_DIM)
    gating = jax.nn.sigmoid(projected[:, :, 3])
    bias = jnp.dot(flat, att_bias, preferred_element_type=jnp.float32).reshape(RES, RES, HEADS).transpose(2, 0, 1)
    same = (chain[:, None] == chain[None, :]).astype(jnp.float32)
    bias = bias + chain_bias[:, None, None] * same[None] + (valid[None, None, :] - 1.0) * 1000000000.0

    def attend(block):
        block_query, block_keys, block_values = block
        scores = jnp.einsum('ajhd,akhd->ahjk', block_query.astype(jnp.float32), block_keys.astype(jnp.float32)) + bias[None]
        weights = jax.nn.softmax(scores, axis=-1).astype(jnp.bfloat16)
        return jnp.einsum('ahjk,akhd->ajhd', weights.astype(jnp.float32), block_values.astype(jnp.float32))
    attended = lax.map(attend, (query, keys, values)).reshape(RES, RES, spread)
    attended = (attended * gating).astype(jnp.bfloat16)
    update = jnp.dot(attended.reshape(RES * RES, spread), att_out, preferred_element_type=jnp.float32)
    first = pair.astype(jnp.float32) + update.reshape(RES, RES, width)
    mixed = norm(first).astype(jnp.bfloat16).reshape(RES * RES, width)
    mult_width = MULT
    quad = jnp.dot(mixed, mult_in, preferred_element_type=jnp.float32).reshape(RES, RES, 4, mult_width)
    outer = valid[:, None, None] * valid[None, :, None]
    left = (outer * jax.nn.sigmoid(quad[:, :, 1]) * quad[:, :, 0]).astype(jnp.bfloat16)
    right = (outer * jax.nn.sigmoid(quad[:, :, 3]) * quad[:, :, 2]).astype(jnp.bfloat16)
    blocks = N_COL * N_SUB
    block_width = RES // blocks

    def accumulate(index, total):
        start = (index * block_width).astype(jnp.int32)
        left_block = lax.dynamic_slice_in_dim(left, start, block_width, 1).astype(jnp.float32)
        right_block = lax.dynamic_slice_in_dim(right, start, block_width, 1).astype(jnp.float32)
        partial_value = jnp.einsum('ikc,jkc->ijc', left_block, right_block).astype(jnp.bfloat16)
        partial_value = lax.optimization_barrier(partial_value)
        return total + partial_value.astype(jnp.float32)
    tri = lax.fori_loop(jnp.int32(0), jnp.int32(blocks), accumulate, jnp.zeros((RES, RES, mult_width), jnp.float32))
    gate_out = jax.nn.sigmoid(jnp.dot(mixed, mult_gate, preferred_element_type=jnp.float32))
    tri_normed = norm(tri).astype(jnp.bfloat16).reshape(RES * RES, mult_width)
    second = first + (gate_out * jnp.dot(tri_normed, mult_out, preferred_element_type=jnp.float32)).reshape(RES, RES, width)
    last_normed = norm(second).astype(jnp.bfloat16).reshape(RES * RES, width)
    hidden = jax.nn.relu(jnp.dot(last_normed, trans_up, preferred_element_type=jnp.float32)).astype(jnp.bfloat16)
    result = second + jnp.dot(hidden, trans_down, preferred_element_type=jnp.float32).reshape(RES, RES, width)
    return result.astype(jnp.bfloat16)
```

```python
import functools

import jax
import jax.numpy as jnp
from jax import lax
from jax.experimental import pallas as pl
from jax.experimental.pallas import tpu as pltpu
from jax.sharding import PartitionSpec as P


def norm(value):
    mean = jnp.mean(value, axis=-1, keepdims=True)
    centred = value - mean
    variance = jnp.mean(centred * centred, axis=-1, keepdims=True)
    return centred * lax.rsqrt(variance + 1e-05)


def local(
    pair,
    length,
    chain,
    att_proj,
    att_bias,
    chain_bias,
    att_out,
    mult_in,
    mult_gate,
    mult_out,
    trans_up,
    trans_down,
):
    rows, cols, width = pair.shape
    row_count = lax.axis_size("row")
    sub_count = lax.axis_size("sub")
    row_index = lax.axis_index("row")
    col_index = lax.axis_index("col")
    sub_index = lax.axis_index("sub")
    total = rows * row_count
    half = cols // sub_count
    heads_here = att_bias.shape[1]
    spread = att_out.shape[0]
    head_dim = spread // heads_here
    mult_width = mult_out.shape[0]
    valid = (jnp.arange(total) < length[0]).astype(jnp.float32)
    normed = norm(pair.astype(jnp.float32)).astype(jnp.bfloat16)
    flat = normed.reshape(rows * cols, width)
    projected = jnp.dot(
        flat, att_proj.reshape(width, 4 * spread), preferred_element_type=jnp.float32
    ).reshape(rows, cols, 4, spread)
    query = (projected[:, :, 0] * head_dim ** (-0.5)).astype(jnp.bfloat16)
    keys = projected[:, :, 1].astype(jnp.bfloat16)
    values = projected[:, :, 2].astype(jnp.bfloat16)
    gating = jax.nn.sigmoid(projected[:, :, 3])
    bias_local = (
        jnp.dot(flat, att_bias, preferred_element_type=jnp.float32)
        .reshape(rows, cols, heads_here)
        .transpose(2, 0, 1)
    )
    keys_all, values_all = (
        lax.all_gather(keys, "col", axis=1, tiled=True),
        lax.all_gather(values, "col", axis=1, tiled=True),
    )
    column_bias = lax.all_gather(bias_local, "row", axis=1, tiled=True)
    bias_here = lax.all_to_all(column_bias, "col", split_axis=1, concat_axis=2, tiled=True)
    chain_here = lax.dynamic_slice_in_dim(chain, col_index * cols, cols, 0)
    same = (chain_here[:, None] == chain[None, :]).astype(jnp.float32)
    bias_here = (
        bias_here
        + chain_bias[:, None, None] * same[None]
        + (valid[None, None, :] - 1.0) * 1000000000.0
    )

    def attend(block):
        block_query, block_keys, block_values = block
        scores = (
            jnp.einsum(
                "ajhd,akhd->ahjk", block_query, block_keys, preferred_element_type=jnp.float32
            )
            + bias_here[None]
        )
        weights = jax.nn.softmax(scores, axis=-1).astype(jnp.bfloat16)
        return jnp.einsum(
            "ahjk,akhd->ajhd", weights, block_values, preferred_element_type=jnp.float32
        )

    attended = lax.map(
        attend,
        (
            query.reshape(rows // 2, 2, cols, heads_here, head_dim),
            keys_all.reshape(rows // 2, 2, total, heads_here, head_dim),
            values_all.reshape(rows // 2, 2, total, heads_here, head_dim),
        ),
    )
    attended = (attended.reshape(rows, cols, spread) * gating).astype(jnp.bfloat16)
    update = jnp.dot(
        attended.reshape(rows * cols, spread), att_out, preferred_element_type=jnp.float32
    ).reshape(rows, cols, width)
    update_half = lax.psum_scatter(
        update.astype(jnp.bfloat16), "sub", scatter_dimension=1, tiled=True
    ).astype(jnp.float32)
    pair_half = lax.dynamic_slice_in_dim(pair, sub_index * half, half, 1).astype(jnp.float32)
    first = pair_half + update_half
    mixed = norm(first).astype(jnp.bfloat16)
    mixed_flat = mixed.reshape(rows * half, width)
    quad = jnp.dot(mixed_flat, mult_in, preferred_element_type=jnp.float32).reshape(
        rows, half, 4, mult_width
    )
    row_valid = lax.dynamic_slice_in_dim(valid, row_index * rows, rows, 0)
    col_valid = lax.dynamic_slice_in_dim(valid, col_index * cols + sub_index * half, half, 0)
    outer = row_valid[:, None, None] * col_valid[None, :, None]
    left = (outer * jax.nn.sigmoid(quad[:, :, 1]) * quad[:, :, 0]).astype(jnp.bfloat16)
    right = (outer * jax.nn.sigmoid(quad[:, :, 3]) * quad[:, :, 2]).astype(jnp.bfloat16)
    gate_out = jax.nn.sigmoid(jnp.dot(mixed_flat, mult_gate, preferred_element_type=jnp.float32))
    partial_value = jnp.einsum(
        "ikc,jkc->ijc",
        left,
        lax.all_gather(right, "row", axis=0, tiled=True),
        preferred_element_type=jnp.float32,
    )
    tri = lax.psum_scatter(
        partial_value.astype(jnp.bfloat16), ("col", "sub"), scatter_dimension=1, tiled=True
    ).astype(jnp.float32)
    tri_normed = norm(tri).astype(jnp.bfloat16).reshape(rows * half, mult_width)
    second = first + (
        gate_out * jnp.dot(tri_normed, mult_out, preferred_element_type=jnp.float32)
    ).reshape(rows, half, width)
    last_normed = norm(second).astype(jnp.bfloat16).reshape(rows * half, width)
    hidden = jax.nn.relu(jnp.dot(last_normed, trans_up, preferred_element_type=jnp.float32)).astype(
        jnp.bfloat16
    )
    result = second + jnp.dot(hidden, trans_down, preferred_element_type=jnp.float32).reshape(
        rows, half, width
    )
    return result.astype(jnp.bfloat16)


NT = (((1,), (1,)), ((), ()))
TN = (((0,), (0,)), ((), ()))
F32 = jnp.float32
BF16 = jnp.bfloat16
STEPS = (((0, 1), (2, 1)), ((3, 1), (1, 1)), ((1, 0), (1, 0)), ((2, 0), (3, 0)))


def replicated(mesh):
    shape = mesh.shape
    return shape["row"] == 4 and shape["col"] == 2 and shape["sub"] == 2


def dot(left, right, dims=(((1,), (0,)), ((), ()))):
    return lax.dot_general(left, right, dims, preferred_element_type=F32)


def fused(
    length_ref,
    chain_bias_ref,
    chain_ref,
    own_ref,
    *refs,
    rows,
    cols,
    heads,
    head_dim,
    tokens,
    sources,
):
    count = len(sources)
    block_refs = refs[:count]
    (
        proj_own_ref,
        proj_other_ref,
        att_bias_ref,
        out_own_ref,
        out_other_ref,
        mult_in_ref,
        mult_gate_ref,
        mult_out_ref,
        trans_up_ref,
        trans_down_ref,
        result_ref,
        normed_ref,
        raw_ref,
        turn_ref,
        bias_ref,
        left_ref,
        right_ref,
        first_ref,
        tile_ref,
    ) = refs[count:]
    width = own_ref.shape[-1]
    total = normed_ref.shape[0]
    wide = normed_ref.shape[1]
    row_index = lax.axis_index("row")
    col_index = lax.axis_index("col")
    sub_index = lax.axis_index("sub")
    other_rows = col_index * lax.axis_size("sub") + sub_index
    length = length_ref[0]

    normed_ref[:, total:, :] = jnp.zeros((total, wide - total, width), F32)

    def place(ref, row_block, col_block):
        value = ref[...].astype(F32)
        at = (pl.ds(row_block * rows, rows), pl.ds(pl.multiple_of(col_block * cols, 8), cols))
        raw_ref[at[0], at[1], :] = value
        normed_ref[at[0], at[1], :] = norm(value)

    place(own_ref, row_index, col_index)
    for ref, (row_step, col_step) in zip(block_refs, sources):
        row_off = jnp.where(sub_index == 0, row_step[0], row_step[1])
        col_off = jnp.where(sub_index == 0, col_step[0], col_step[1])
        place(ref, row_index ^ row_off, col_index ^ col_off)

    def pair_tokens(start):
        return normed_ref[pl.ds(start, 2)].reshape(2 * wide, width).astype(BF16)

    att_bias = att_bias_ref[...]
    for index in range(total // 2):
        both = dot(att_bias, pair_tokens(2 * index), NT)
        turn_ref[2 * index] = both
        turn_ref[2 * index + 1] = pltpu.roll(both, wide, 1)
    chain_row = jnp.broadcast_to(chain_ref[...].astype(F32), (2 * wide, 2 * wide))
    same = (chain_row == chain_row.T).astype(F32)[:total]
    key_place = lax.broadcasted_iota(jnp.int32, (total, 2 * wide), 1)
    masked = jnp.where(key_place < length, 0.0, -1000000000.0)
    for head in range(heads):
        value = turn_ref[:, head, :] + chain_bias_ref[head] * same + masked
        value = jnp.concatenate([value, jnp.zeros((wide - total, 2 * wide), F32)], axis=0)
        value = jnp.concatenate([value, value], axis=0).T
        bias_ref[pl.ds(head * total, total)] = value[:total]

    def joined(own, other, part):
        return jnp.concatenate([own[part], other[part]], axis=0)

    key_weights = joined(proj_own_ref, proj_other_ref, 1)
    turned_weights = jnp.concatenate(
        [joined(proj_own_ref, proj_other_ref, part) for part in (0, 2, 3)], axis=0
    )
    out_weights = jnp.concatenate([out_own_ref[...], out_other_ref[...]], axis=0)
    lane = lax.broadcasted_iota(jnp.int32, (1, 2 * wide), 1)
    lane_first = (lane < wide).astype(BF16)
    lane_second = (lane >= wide).astype(BF16)
    channel = lax.broadcasted_iota(jnp.int32, (1, width), 1)
    head_masks = [
        ((channel >= head * head_dim) & (channel < (head + 1) * head_dim)).astype(BF16)
        for head in range(heads)
    ]
    pad = jnp.zeros((wide - total, 2 * wide), BF16)

    def attend(start):
        flat = pair_tokens(start)
        turned = dot(turned_weights, flat, NT)
        query = (turned[:width] * head_dim ** (-0.5)).astype(BF16)
        values = turned[width : 2 * width].astype(BF16)
        gating = jax.nn.sigmoid(turned[2 * width :])
        keys = dot(flat, key_weights, NT).astype(BF16)
        spread_keys = jnp.concatenate(
            [
                jnp.concatenate(
                    [keys[at : at + total] * mask for mask in head_masks], axis=0
                )
                for at in (0, wide)
            ],
            axis=1,
        )
        spread_query = jnp.concatenate([query * lane_first, query * lane_second], axis=0)
        scores = dot(spread_keys, spread_query) + bias_ref[...]
        attended = []
        for head in range(heads):
            part = scores[head * total : (head + 1) * total]
            part = jnp.exp(part - jnp.max(part, axis=0, keepdims=True))
            weights = (part / jnp.sum(part, axis=0, keepdims=True)).astype(BF16)
            spread_weights = jnp.concatenate(
                [weights * lane_first, pad, weights * lane_second, pad], axis=0
            )
            attended.append(
                dot(values[head * head_dim : (head + 1) * head_dim], spread_weights)
            )
        attended = (jnp.concatenate(attended, axis=0) * gating).astype(BF16)
        update = dot(attended, out_weights, TN)
        return raw_ref[pl.ds(start, 2)].reshape(2 * wide, width) + update

    col_valid = (lax.broadcasted_iota(jnp.int32, (total, width), 0) < length).astype(F32)

    def halves(start, step, first, into_ref, column):
        mixed = norm(first).astype(BF16)
        both = dot(mixed, mult_in_ref[:, column : column + 2 * width])
        side = jax.nn.sigmoid(both[:, width:]) * both[:, :width]
        for which in range(2):
            row_valid = (start + which < length).astype(F32)
            value = side[which * wide : which * wide + total] * (col_valid * row_valid)
            into_ref[2 * step + which] = value.astype(BF16).astype(F32)

    def own_step(step, carry):
        start = row_index * rows + 2 * step
        first = attend(start)
        first_ref[pl.ds(2 * step, 2)] = first.reshape(2, wide, width)
        halves(start, step, first, left_ref, 0)
        return carry

    def other_step(step, carry):
        start = other_rows * rows + 2 * step
        halves(start, step, attend(start), right_ref, 2 * width)
        return carry

    lax.fori_loop(0, rows // 2, own_step, 0)
    lax.fori_loop(0, rows // 2, other_step, 0)

    half = rows
    for block in range(total // half):

        @pl.when(other_rows == block)
        def _():
            tile_ref[:, :half, :] = first_ref[:, block * half : (block + 1) * half, :]

    def triangle(step, carry):
        left = left_ref[step]
        sums = [
            jnp.sum(left * right_ref[other], axis=0, keepdims=True) for other in range(half)
        ]
        first_ref[step, :half, :] = jnp.concatenate(sums, axis=0)
        return carry

    lax.fori_loop(0, rows, triangle, 0)
    deep = tile_ref.shape[1]
    first = tile_ref[...].reshape(rows * deep, width)
    tri = first_ref[:, :deep, :].reshape(rows * deep, width)
    mixed = norm(first).astype(BF16)
    gate = jax.nn.sigmoid(dot(mixed, mult_gate_ref[...]))
    second = first + gate * dot(norm(tri).astype(BF16), mult_out_ref[...])
    hidden = jax.nn.relu(dot(norm(second).astype(BF16), trans_up_ref[...])).astype(BF16)
    result = second + dot(hidden, trans_down_ref[...])
    result_ref[...] = result.astype(BF16).reshape(rows, deep, width)[:, :half, :]


def gathered(
    pair,
    length,
    chain,
    att_proj,
    att_bias,
    chain_bias,
    att_out,
    mult_in,
    mult_gate,
    mult_out,
    trans_up,
    trans_down,
):
    rows, cols, width = pair.shape
    row_count = lax.axis_size("row")
    col_count = lax.axis_size("col")
    sub_count = lax.axis_size("sub")
    total = rows * row_count
    heads = att_bias.shape[1] * sub_count
    head_dim = att_out.shape[0] // att_bias.shape[1]
    axes = ("row", "col", "sub")

    def place(row, col, sub):
        return (row * col_count + col) * sub_count + sub

    def exchange(value, offsets):
        routes = [
            (place(row, col, sub), place(row ^ offsets[sub][0], col ^ offsets[sub][1], sub))
            for row in range(row_count)
            for col in range(col_count)
            for sub in range(sub_count)
        ]
        return lax.ppermute(value, axes, routes)

    swap = functools.partial(lax.ppermute, axis_name="sub", perm=[(0, 1), (1, 0)])
    proj_other = swap(att_proj)
    out_other = swap(att_out)
    bias_other = swap(att_bias)
    chain_other = swap(chain_bias)
    blocks, sources = [], []
    fetched = [exchange(pair, offsets) for offsets in STEPS]
    for value, offsets in zip(fetched, STEPS):
        mine = tuple(zip(offsets[0], offsets[1]))
        blocks.append(value)
        sources.append(mine)
        if offsets[0] != offsets[1]:
            blocks.append(swap(value))
            sources.append(tuple((b, a) for a, b in mine))
    att_bias_rows = jnp.concatenate([att_bias.T, bias_other.T], axis=0)
    att_bias_rows = jnp.pad(att_bias_rows, ((0, 8 - heads), (0, 0)))
    wide = 64
    deep = 16
    smem = pl.BlockSpec(memory_space=pltpu.SMEM)
    vmem = pl.BlockSpec(memory_space=pltpu.VMEM)
    operands = [
        length,
        jnp.concatenate([chain_bias, chain_other]),
        jnp.pad(chain, (0, 2 * wide - total)).reshape(1, 2 * wide),
        pair,
        *blocks,
        att_proj.transpose(1, 2, 0),
        proj_other.transpose(1, 2, 0),
        att_bias_rows,
        att_out,
        out_other,
        mult_in,
        mult_gate,
        mult_out,
        trans_up,
        trans_down,
    ]
    return pl.pallas_call(
        functools.partial(
            fused,
            rows=rows,
            cols=cols,
            heads=heads,
            head_dim=head_dim,
            tokens=wide,
            sources=tuple(sources),
        ),
        out_shape=jax.ShapeDtypeStruct((rows, cols // sub_count, width), jnp.bfloat16),
        in_specs=[smem, smem] + [vmem] * (len(operands) - 2),
        out_specs=vmem,
        scratch_shapes=[
            pltpu.VMEM((total, wide, width), F32),
            pltpu.VMEM((total, wide, width), F32),
            pltpu.VMEM((total, 8, 2 * wide), F32),
            pltpu.VMEM((heads * total, 2 * wide), F32),
            pltpu.VMEM((rows, total, width), F32),
            pltpu.VMEM((rows, total, width), F32),
            pltpu.VMEM((rows, wide, width), F32),
            pltpu.VMEM((rows, deep, width), F32),
        ],
        compiler_params=pltpu.CompilerParams(vmem_limit_bytes=48 * 1024 * 1024),
    )(*operands)


def solution(mesh):
    placed = (
        P(("grp", "row"), "col", None),
        P("grp"),
        P("grp"),
        P(None, None, "sub"),
        P(None, "sub"),
        P("sub"),
        P("sub", None),
        P(),
        P(),
        P(),
        P(),
        P(),
    )
    fits = replicated(mesh)
    return jax.shard_map(
        gathered if fits else local,
        mesh=mesh,
        in_specs=placed,
        out_specs=P(("grp", "row"), ("col", "sub"), None),
        check_vma=False,
    )
```

```python
import functools

import jax
import jax.numpy as jnp
from jax import lax
from jax.experimental import pallas as pl
from jax.experimental.pallas import tpu as pltpu
from jax.sharding import PartitionSpec as P


def norm(value):
    mean = jnp.mean(value, axis=-1, keepdims=True)
    centred = value - mean
    variance = jnp.mean(centred * centred, axis=-1, keepdims=True)
    return centred * lax.rsqrt(variance + 1e-05)


def local(
    pair,
    length,
    chain,
    att_proj,
    att_bias,
    chain_bias,
    att_out,
    mult_in,
    mult_gate,
    mult_out,
    trans_up,
    trans_down,
):
    rows, cols, width = pair.shape
    row_count = lax.axis_size("row")
    sub_count = lax.axis_size("sub")
    row_index = lax.axis_index("row")
    col_index = lax.axis_index("col")
    sub_index = lax.axis_index("sub")
    total = rows * row_count
    half = cols // sub_count
    heads_here = att_bias.shape[1]
    spread = att_out.shape[0]
    head_dim = spread // heads_here
    mult_width = mult_out.shape[0]
    valid = (jnp.arange(total) < length[0]).astype(jnp.float32)
    normed = norm(pair.astype(jnp.float32)).astype(jnp.bfloat16)
    flat = normed.reshape(rows * cols, width)
    projected = jnp.dot(
        flat, att_proj.reshape(width, 4 * spread), preferred_element_type=jnp.float32
    ).reshape(rows, cols, 4, spread)
    query = (projected[:, :, 0] * head_dim ** (-0.5)).astype(jnp.bfloat16)
    keys = projected[:, :, 1].astype(jnp.bfloat16)
    values = projected[:, :, 2].astype(jnp.bfloat16)
    gating = jax.nn.sigmoid(projected[:, :, 3])
    bias_local = (
        jnp.dot(flat, att_bias, preferred_element_type=jnp.float32)
        .reshape(rows, cols, heads_here)
        .transpose(2, 0, 1)
    )
    keys_all, values_all = (
        lax.all_gather(keys, "col", axis=1, tiled=True),
        lax.all_gather(values, "col", axis=1, tiled=True),
    )
    column_bias = lax.all_gather(bias_local, "row", axis=1, tiled=True)
    bias_here = lax.all_to_all(column_bias, "col", split_axis=1, concat_axis=2, tiled=True)
    chain_here = lax.dynamic_slice_in_dim(chain, col_index * cols, cols, 0)
    same = (chain_here[:, None] == chain[None, :]).astype(jnp.float32)
    bias_here = (
        bias_here
        + chain_bias[:, None, None] * same[None]
        + (valid[None, None, :] - 1.0) * 1000000000.0
    )

    def attend(block):
        block_query, block_keys, block_values = block
        scores = (
            jnp.einsum(
                "ajhd,akhd->ahjk", block_query, block_keys, preferred_element_type=jnp.float32
            )
            + bias_here[None]
        )
        weights = jax.nn.softmax(scores, axis=-1).astype(jnp.bfloat16)
        return jnp.einsum(
            "ahjk,akhd->ajhd", weights, block_values, preferred_element_type=jnp.float32
        )

    attended = lax.map(
        attend,
        (
            query.reshape(rows // 2, 2, cols, heads_here, head_dim),
            keys_all.reshape(rows // 2, 2, total, heads_here, head_dim),
            values_all.reshape(rows // 2, 2, total, heads_here, head_dim),
        ),
    )
    attended = (attended.reshape(rows, cols, spread) * gating).astype(jnp.bfloat16)
    update = jnp.dot(
        attended.reshape(rows * cols, spread), att_out, preferred_element_type=jnp.float32
    ).reshape(rows, cols, width)
    update_half = lax.psum_scatter(
        update.astype(jnp.bfloat16), "sub", scatter_dimension=1, tiled=True
    ).astype(jnp.float32)
    pair_half = lax.dynamic_slice_in_dim(pair, sub_index * half, half, 1).astype(jnp.float32)
    first = pair_half + update_half
    mixed = norm(first).astype(jnp.bfloat16)
    mixed_flat = mixed.reshape(rows * half, width)
    quad = jnp.dot(mixed_flat, mult_in, preferred_element_type=jnp.float32).reshape(
        rows, half, 4, mult_width
    )
    row_valid = lax.dynamic_slice_in_dim(valid, row_index * rows, rows, 0)
    col_valid = lax.dynamic_slice_in_dim(valid, col_index * cols + sub_index * half, half, 0)
    outer = row_valid[:, None, None] * col_valid[None, :, None]
    left = (outer * jax.nn.sigmoid(quad[:, :, 1]) * quad[:, :, 0]).astype(jnp.bfloat16)
    right = (outer * jax.nn.sigmoid(quad[:, :, 3]) * quad[:, :, 2]).astype(jnp.bfloat16)
    gate_out = jax.nn.sigmoid(jnp.dot(mixed_flat, mult_gate, preferred_element_type=jnp.float32))
    partial_value = jnp.einsum(
        "ikc,jkc->ijc",
        left,
        lax.all_gather(right, "row", axis=0, tiled=True),
        preferred_element_type=jnp.float32,
    )
    tri = lax.psum_scatter(
        partial_value.astype(jnp.bfloat16), ("col", "sub"), scatter_dimension=1, tiled=True
    ).astype(jnp.float32)
    tri_normed = norm(tri).astype(jnp.bfloat16).reshape(rows * half, mult_width)
    second = first + (
        gate_out * jnp.dot(tri_normed, mult_out, preferred_element_type=jnp.float32)
    ).reshape(rows, half, width)
    last_normed = norm(second).astype(jnp.bfloat16).reshape(rows * half, width)
    hidden = jax.nn.relu(jnp.dot(last_normed, trans_up, preferred_element_type=jnp.float32)).astype(
        jnp.bfloat16
    )
    result = second + jnp.dot(hidden, trans_down, preferred_element_type=jnp.float32).reshape(
        rows, half, width
    )
    return result.astype(jnp.bfloat16)


NT = (((1,), (1,)), ((), ()))
TN = (((0,), (0,)), ((), ()))
F32 = jnp.float32
BF16 = jnp.bfloat16
UNROLL = 6
STEPS = (((0, 1), (2, 1)), ((3, 1), (1, 1)), ((1, 0), (1, 0)), ((2, 0), (3, 0)))


def replicated(mesh):
    shape = mesh.shape
    return shape["row"] == 4 and shape["col"] == 2 and shape["sub"] == 2


def dot(left, right, dims=(((1,), (0,)), ((), ()))):
    return lax.dot_general(left, right, dims, preferred_element_type=F32)


def fused(
    length_ref,
    chain_bias_ref,
    chain_ref,
    own_ref,
    *refs,
    rows,
    cols,
    heads,
    head_dim,
    tokens,
    sources,
):
    count = len(sources)
    block_refs = refs[:count]
    (
        proj_own_ref,
        proj_other_ref,
        att_bias_ref,
        out_own_ref,
        out_other_ref,
        *kept_refs,
        result_ref,
        mult_in_ref,
        mult_gate_ref,
        mult_out_ref,
        trans_up_ref,
        trans_down_ref,
        copy_sems,
        normed_ref,
        raw_ref,
        turn_ref,
        bias_ref,
        left_ref,
        right_ref,
        first_ref,
        tile_ref,
    ) = refs[count:]
    copies = [
        pltpu.make_async_copy(kept, held, copy_sems.at[at])
        for at, (kept, held) in enumerate(
            zip(
                kept_refs,
                (mult_in_ref, mult_gate_ref, mult_out_ref, trans_up_ref, trans_down_ref),
            )
        )
    ]
    for copy in copies:
        copy.start()
    width = own_ref.shape[-1]
    total = normed_ref.shape[0]
    wide = normed_ref.shape[1]
    row_index = lax.axis_index("row")
    col_index = lax.axis_index("col")
    sub_index = lax.axis_index("sub")
    other_rows = col_index * lax.axis_size("sub") + sub_index
    length = length_ref[0]

    normed_ref[:, total:, :] = jnp.zeros((total, wide - total, width), F32)

    def place(ref, row_block, col_block):
        value = ref[...].astype(F32)
        at = (pl.ds(row_block * rows, rows), pl.ds(pl.multiple_of(col_block * cols, 8), cols))
        raw_ref[at[0], at[1], :] = value
        normed_ref[at[0], at[1], :] = norm(value)

    place(own_ref, row_index, col_index)
    for ref, (row_step, col_step) in zip(block_refs, sources):
        row_off = jnp.where(sub_index == 0, row_step[0], row_step[1])
        col_off = jnp.where(sub_index == 0, col_step[0], col_step[1])
        place(ref, row_index ^ row_off, col_index ^ col_off)

    def pair_tokens(start):
        return normed_ref[pl.ds(start, 2)].reshape(2 * wide, width).astype(BF16)

    att_bias = att_bias_ref[...]
    for index in range(total // 2):
        both = dot(att_bias, pair_tokens(2 * index), NT)
        turn_ref[2 * index] = both
        turn_ref[2 * index + 1] = pltpu.roll(both, wide, 1)
    chain_row = jnp.broadcast_to(chain_ref[...].astype(F32), (2 * wide, 2 * wide))
    same = (chain_row == chain_row.T).astype(F32)[:total]
    key_place = lax.broadcasted_iota(jnp.int32, (total, 2 * wide), 1)
    masked = jnp.where(key_place < length, 0.0, -1000000000.0)
    for head in range(heads):
        value = turn_ref[:, head, :] + chain_bias_ref[head] * same + masked
        value = jnp.concatenate([value, jnp.zeros((wide - total, 2 * wide), F32)], axis=0)
        value = jnp.concatenate([value, value], axis=0).T
        bias_ref[pl.ds(head * total, total)] = value[:total]

    def joined(own, other, part):
        return jnp.concatenate([own[part], other[part]], axis=0)

    key_weights = joined(proj_own_ref, proj_other_ref, 1)
    turned_weights = jnp.concatenate(
        [joined(proj_own_ref, proj_other_ref, part) for part in (0, 2, 3)], axis=0
    )
    out_weights = jnp.concatenate([out_own_ref[...], out_other_ref[...]], axis=0)
    lane = lax.broadcasted_iota(jnp.int32, (1, 2 * wide), 1)
    lane_first = (lane < wide).astype(BF16)
    lane_second = (lane >= wide).astype(BF16)
    channel = lax.broadcasted_iota(jnp.int32, (1, width), 1)
    head_masks = [
        ((channel >= head * head_dim) & (channel < (head + 1) * head_dim)).astype(BF16)
        for head in range(heads)
    ]
    pad = jnp.zeros((wide - total, 2 * wide), BF16)

    def attend(starts):
        flats = [pair_tokens(start) for start in starts]
        turned = [dot(turned_weights, flat, NT) for flat in flats]
        keys = [dot(flat, key_weights, NT).astype(BF16) for flat in flats]
        scores = []
        for key, turn in zip(keys, turned):
            query = (turn[:width] * head_dim ** (-0.5)).astype(BF16)
            spread_keys = jnp.concatenate(
                [
                    jnp.concatenate(
                        [key[at : at + total] * mask for mask in head_masks], axis=0
                    )
                    for at in (0, wide)
                ],
                axis=1,
            )
            spread_query = jnp.concatenate([query * lane_first, query * lane_second], axis=0)
            scores.append(dot(spread_keys, spread_query))
        attended = []
        for score, turn in zip(scores, turned):
            values = turn[width : 2 * width].astype(BF16)
            parts = []
            for head in range(heads):
                rows_of = slice(head * total, (head + 1) * total)
                part = score[rows_of] + bias_ref[rows_of]
                part = jnp.exp(part - jnp.max(part, axis=0, keepdims=True))
                weights = (part / jnp.sum(part, axis=0, keepdims=True)).astype(BF16)
                spread_weights = jnp.concatenate(
                    [weights * lane_first, pad, weights * lane_second, pad], axis=0
                )
                parts.append(
                    dot(values[head * head_dim : (head + 1) * head_dim], spread_weights)
                )
            gating = jax.nn.sigmoid(turn[2 * width :])
            attended.append((jnp.concatenate(parts, axis=0) * gating).astype(BF16))
        return [
            raw_ref[pl.ds(start, 2)].reshape(2 * wide, width) + dot(value, out_weights, TN)
            for start, value in zip(starts, attended)
        ]

    col_valid = (lax.broadcasted_iota(jnp.int32, (total, width), 0) < length).astype(F32)

    def halves(start, step, first, into_ref, column):
        mixed = norm(first).astype(BF16)
        both = dot(mixed, mult_in_ref[:, column : column + 2 * width])
        side = jax.nn.sigmoid(both[:, width:]) * both[:, :width]
        for which in range(2):
            row_valid = (start + which < length).astype(F32)
            value = side[which * wide : which * wide + total] * (col_valid * row_valid)
            into_ref[2 * step + which] = value.astype(BF16).astype(F32)

    def group(step, carry):
        steps = [step * UNROLL + at for at in range(UNROLL)]
        own = [row_index * rows + 2 * at for at in steps]
        others = [other_rows * rows + 2 * at for at in steps]
        firsts = attend(own + others)
        for at, start, first in zip(steps, own, firsts):
            first_ref[pl.ds(2 * at, 2)] = first.reshape(2, wide, width)
            halves(start, at, first, left_ref, 0)
        for at, start, first in zip(steps, others, firsts[UNROLL:]):
            halves(start, at, first, right_ref, 2 * width)
        return carry

    for copy in copies[:1]:
        copy.wait()
    lax.fori_loop(0, rows // 2 // UNROLL, group, 0)

    half = rows
    for block in range(total // half):

        @pl.when(other_rows == block)
        def _():
            tile_ref[:, :half, :] = first_ref[:, block * half : (block + 1) * half, :]

    def triangle(step, carry):
        left = left_ref[step]
        sums = [
            jnp.sum(left * right_ref[other], axis=0, keepdims=True) for other in range(half)
        ]
        first_ref[step, :half, :] = jnp.concatenate(sums, axis=0)
        return carry

    lax.fori_loop(0, rows, triangle, 0)
    for copy in copies[1:]:
        copy.wait()
    deep = tile_ref.shape[1]
    first = tile_ref[...].reshape(rows * deep, width)
    tri = first_ref[:, :deep, :].reshape(rows * deep, width)
    mixed = norm(first).astype(BF16)
    gate = jax.nn.sigmoid(dot(mixed, mult_gate_ref[...]))
    second = first + gate * dot(norm(tri).astype(BF16), mult_out_ref[...])
    hidden = jax.nn.relu(dot(norm(second).astype(BF16), trans_up_ref[...])).astype(BF16)
    result = second + dot(hidden, trans_down_ref[...])
    result_ref[...] = result.astype(BF16).reshape(rows, deep, width)[:, :half, :]


def gathered(
    pair,
    length,
    chain,
    att_proj,
    att_bias,
    chain_bias,
    att_out,
    mult_in,
    mult_gate,
    mult_out,
    trans_up,
    trans_down,
):
    rows, cols, width = pair.shape
    row_count = lax.axis_size("row")
    col_count = lax.axis_size("col")
    sub_count = lax.axis_size("sub")
    total = rows * row_count
    heads = att_bias.shape[1] * sub_count
    head_dim = att_out.shape[0] // att_bias.shape[1]
    axes = ("row", "col", "sub")

    def place(row, col, sub):
        return (row * col_count + col) * sub_count + sub

    def exchange(value, offsets):
        routes = [
            (place(row, col, sub), place(row ^ offsets[sub][0], col ^ offsets[sub][1], sub))
            for row in range(row_count)
            for col in range(col_count)
            for sub in range(sub_count)
        ]
        return lax.ppermute(value, axes, routes)

    swap = functools.partial(lax.ppermute, axis_name="sub", perm=[(0, 1), (1, 0)])
    proj_other = swap(att_proj)
    out_other = swap(att_out)
    bias_other = swap(att_bias)
    chain_other = swap(chain_bias)
    blocks, sources = [], []
    fetched = [exchange(pair, offsets) for offsets in STEPS]
    for value, offsets in zip(fetched, STEPS):
        mine = tuple(zip(offsets[0], offsets[1]))
        blocks.append(value)
        sources.append(mine)
        if offsets[0] != offsets[1]:
            blocks.append(swap(value))
            sources.append(tuple((b, a) for a, b in mine))
    att_bias_rows = jnp.concatenate([att_bias.T, bias_other.T], axis=0)
    att_bias_rows = jnp.pad(att_bias_rows, ((0, 8 - heads), (0, 0)))
    wide = 64
    deep = 16
    smem = pl.BlockSpec(memory_space=pltpu.SMEM)
    vmem = pl.BlockSpec(memory_space=pltpu.VMEM)
    hbm = pl.BlockSpec(memory_space=pltpu.HBM)
    operands = [
        length,
        jnp.concatenate([chain_bias, chain_other]),
        jnp.pad(chain, (0, 2 * wide - total)).reshape(1, 2 * wide),
        pair,
        *blocks,
        att_proj.transpose(1, 2, 0),
        proj_other.transpose(1, 2, 0),
        att_bias_rows,
        att_out,
        out_other,
        mult_in,
        mult_gate,
        mult_out,
        trans_up,
        trans_down,
    ]
    return pl.pallas_call(
        functools.partial(
            fused,
            rows=rows,
            cols=cols,
            heads=heads,
            head_dim=head_dim,
            tokens=wide,
            sources=tuple(sources),
        ),
        out_shape=jax.ShapeDtypeStruct((rows, cols // sub_count, width), jnp.bfloat16),
        in_specs=[smem, smem] + [vmem] * (len(operands) - 7) + [hbm] * 5,
        out_specs=vmem,
        scratch_shapes=[
            *[pltpu.VMEM(each.shape, each.dtype) for each in operands[-5:]],
            pltpu.SemaphoreType.DMA((5,)),
            pltpu.VMEM((total, wide, width), F32),
            pltpu.VMEM((total, wide, width), F32),
            pltpu.VMEM((total, 8, 2 * wide), F32),
            pltpu.VMEM((heads * total, 2 * wide), F32),
            pltpu.VMEM((rows, total, width), F32),
            pltpu.VMEM((rows, total, width), F32),
            pltpu.VMEM((rows, wide, width), F32),
            pltpu.VMEM((rows, deep, width), F32),
        ],
        compiler_params=pltpu.CompilerParams(vmem_limit_bytes=48 * 1024 * 1024),
    )(*operands)


def solution(mesh):
    placed = (
        P(("grp", "row"), "col", None),
        P("grp"),
        P("grp"),
        P(None, None, "sub"),
        P(None, "sub"),
        P("sub"),
        P("sub", None),
        P(),
        P(),
        P(),
        P(),
        P(),
    )
    fits = replicated(mesh)
    return jax.shard_map(
        gathered if fits else local,
        mesh=mesh,
        in_specs=placed,
        out_specs=P(("grp", "row"), ("col", "sub"), None),
        check_vma=False,
    )
```

```python
import functools

import jax
import jax.numpy as jnp
from jax import lax
from jax.experimental import pallas as pl
from jax.experimental.pallas import tpu as pltpu
from jax.sharding import PartitionSpec as P


def norm(value):
    mean = jnp.mean(value, axis=-1, keepdims=True)
    centred = value - mean
    variance = jnp.mean(centred * centred, axis=-1, keepdims=True)
    return centred * lax.rsqrt(variance + 1e-05)


def local(
    pair,
    length,
    chain,
    att_proj,
    att_bias,
    chain_bias,
    att_out,
    mult_in,
    mult_gate,
    mult_out,
    trans_up,
    trans_down,
):
    rows, cols, width = pair.shape
    row_count = lax.axis_size("row")
    sub_count = lax.axis_size("sub")
    row_index = lax.axis_index("row")
    col_index = lax.axis_index("col")
    sub_index = lax.axis_index("sub")
    total = rows * row_count
    half = cols // sub_count
    heads_here = att_bias.shape[1]
    spread = att_out.shape[0]
    head_dim = spread // heads_here
    mult_width = mult_out.shape[0]
    valid = (jnp.arange(total) < length[0]).astype(jnp.float32)
    normed = norm(pair.astype(jnp.float32)).astype(jnp.bfloat16)
    flat = normed.reshape(rows * cols, width)
    projected = jnp.dot(
        flat, att_proj.reshape(width, 4 * spread), preferred_element_type=jnp.float32
    ).reshape(rows, cols, 4, spread)
    query = (projected[:, :, 0] * head_dim ** (-0.5)).astype(jnp.bfloat16)
    keys = projected[:, :, 1].astype(jnp.bfloat16)
    values = projected[:, :, 2].astype(jnp.bfloat16)
    gating = jax.nn.sigmoid(projected[:, :, 3])
    bias_local = (
        jnp.dot(flat, att_bias, preferred_element_type=jnp.float32)
        .reshape(rows, cols, heads_here)
        .transpose(2, 0, 1)
    )
    keys_all, values_all = (
        lax.all_gather(keys, "col", axis=1, tiled=True),
        lax.all_gather(values, "col", axis=1, tiled=True),
    )
    column_bias = lax.all_gather(bias_local, "row", axis=1, tiled=True)
    bias_here = lax.all_to_all(column_bias, "col", split_axis=1, concat_axis=2, tiled=True)
    chain_here = lax.dynamic_slice_in_dim(chain, col_index * cols, cols, 0)
    same = (chain_here[:, None] == chain[None, :]).astype(jnp.float32)
    bias_here = (
        bias_here
        + chain_bias[:, None, None] * same[None]
        + (valid[None, None, :] - 1.0) * 1000000000.0
    )

    def attend(block):
        block_query, block_keys, block_values = block
        scores = (
            jnp.einsum(
                "ajhd,akhd->ahjk", block_query, block_keys, preferred_element_type=jnp.float32
            )
            + bias_here[None]
        )
        weights = jax.nn.softmax(scores, axis=-1).astype(jnp.bfloat16)
        return jnp.einsum(
            "ahjk,akhd->ajhd", weights, block_values, preferred_element_type=jnp.float32
        )

    attended = lax.map(
        attend,
        (
            query.reshape(rows // 2, 2, cols, heads_here, head_dim),
            keys_all.reshape(rows // 2, 2, total, heads_here, head_dim),
            values_all.reshape(rows // 2, 2, total, heads_here, head_dim),
        ),
    )
    attended = (attended.reshape(rows, cols, spread) * gating).astype(jnp.bfloat16)
    update = jnp.dot(
        attended.reshape(rows * cols, spread), att_out, preferred_element_type=jnp.float32
    ).reshape(rows, cols, width)
    update_half = lax.psum_scatter(
        update.astype(jnp.bfloat16), "sub", scatter_dimension=1, tiled=True
    ).astype(jnp.float32)
    pair_half = lax.dynamic_slice_in_dim(pair, sub_index * half, half, 1).astype(jnp.float32)
    first = pair_half + update_half
    mixed = norm(first).astype(jnp.bfloat16)
    mixed_flat = mixed.reshape(rows * half, width)
    quad = jnp.dot(mixed_flat, mult_in, preferred_element_type=jnp.float32).reshape(
        rows, half, 4, mult_width
    )
    row_valid = lax.dynamic_slice_in_dim(valid, row_index * rows, rows, 0)
    col_valid = lax.dynamic_slice_in_dim(valid, col_index * cols + sub_index * half, half, 0)
    outer = row_valid[:, None, None] * col_valid[None, :, None]
    left = (outer * jax.nn.sigmoid(quad[:, :, 1]) * quad[:, :, 0]).astype(jnp.bfloat16)
    right = (outer * jax.nn.sigmoid(quad[:, :, 3]) * quad[:, :, 2]).astype(jnp.bfloat16)
    gate_out = jax.nn.sigmoid(jnp.dot(mixed_flat, mult_gate, preferred_element_type=jnp.float32))
    partial_value = jnp.einsum(
        "ikc,jkc->ijc",
        left,
        lax.all_gather(right, "row", axis=0, tiled=True),
        preferred_element_type=jnp.float32,
    )
    tri = lax.psum_scatter(
        partial_value.astype(jnp.bfloat16), ("col", "sub"), scatter_dimension=1, tiled=True
    ).astype(jnp.float32)
    tri_normed = norm(tri).astype(jnp.bfloat16).reshape(rows * half, mult_width)
    second = first + (
        gate_out * jnp.dot(tri_normed, mult_out, preferred_element_type=jnp.float32)
    ).reshape(rows, half, width)
    last_normed = norm(second).astype(jnp.bfloat16).reshape(rows * half, width)
    hidden = jax.nn.relu(jnp.dot(last_normed, trans_up, preferred_element_type=jnp.float32)).astype(
        jnp.bfloat16
    )
    result = second + jnp.dot(hidden, trans_down, preferred_element_type=jnp.float32).reshape(
        rows, half, width
    )
    return result.astype(jnp.bfloat16)


NT = (((1,), (1,)), ((), ()))
TN = (((0,), (0,)), ((), ()))
F32 = jnp.float32
BF16 = jnp.bfloat16
WIDE = 64
GROUP = 6
LIMIT = 16 * 1024 * 1024
STEPS = (((0, 1), (0, 1)), ((3, 1), (2, 1)), ((1, 0), (1, 1)), ((2, 0), (3, 0)))


def replicated(mesh):
    shape = mesh.shape
    return shape["row"] == 4 and shape["col"] == 2 and shape["sub"] == 2


def dot(left, right, dims=(((1,), (0,)), ((), ()))):
    return lax.dot_general(left, right, dims, preferred_element_type=F32)


def flat_pair(ref, start):
    return ref[pl.ds(start, 2)].reshape(2 * ref.shape[1], ref.shape[2])


def head_masks(heads, width):
    channel = lax.broadcasted_iota(jnp.int32, (1, width), 1)
    size = width // heads
    return [
        ((channel >= head * size) & (channel < (head + 1) * size)).astype(BF16)
        for head in range(heads)
    ]


def lane_masks():
    lane = lax.broadcasted_iota(jnp.int32, (1, 2 * WIDE), 1)
    return (lane < WIDE).astype(BF16), (lane >= WIDE).astype(BF16)


def project(tokens, turned_weights, key_weights, heads, total):
    width = tokens[0].shape[1]
    first_lanes, second_lanes = lane_masks()
    masks = head_masks(heads, width)
    turned = [dot(turned_weights, flat, NT) for flat in tokens]
    keys = [dot(flat, key_weights, NT).astype(BF16) for flat in tokens]
    scores = []
    for key, turn in zip(keys, turned):
        query = (turn[:width] * (width // heads) ** (-0.5)).astype(BF16)
        spread_keys = jnp.concatenate(
            [
                jnp.concatenate([key[at : at + total] * mask for mask in masks], axis=0)
                for at in (0, WIDE)
            ],
            axis=1,
        )
        spread_query = jnp.concatenate([query * first_lanes, query * second_lanes], axis=0)
        scores.append(dot(spread_keys, spread_query))
    values = [turn[width : 2 * width].astype(BF16) for turn in turned]
    gates = [jax.nn.sigmoid(turn[2 * width :]) for turn in turned]
    return scores, values, gates


def bias_rows(weights, tokens, turn_ref, row):
    both = dot(weights, tokens, NT)
    turn_ref[row] = both
    turn_ref[row + 1] = pltpu.roll(both, WIDE, 1)


def prepare(
    length_ref,
    chain_hbm,
    own_hbm,
    proj_hbm,
    att_bias_hbm,
    chain_bias_hbm,
    out_hbm,
    mult_in_hbm,
    mult_gate_hbm,
    mult_out_hbm,
    trans_up_hbm,
    trans_down_hbm,
    near_ref,
    proj_other_ref,
    att_bias_other_ref,
    chain_bias_other_ref,
    out_other_ref,
    turned_weights_ref,
    key_weights_ref,
    out_weights_ref,
    att_bias_ref,
    plain_bias_ref,
    valid_ref,
    raw_ref,
    normed_ref,
    scores_ref,
    values_ref,
    gates_ref,
    turn_ref,
    mult_in_ref,
    mult_gate_ref,
    mult_out_ref,
    trans_up_ref,
    trans_down_ref,
    chain_ref,
    own_ref,
    proj_ref,
    att_bias_own_ref,
    chain_bias_ref,
    out_ref,
    copy_sems,
):
    pairs = (
        (own_hbm, own_ref),
        (proj_hbm, proj_ref),
        (chain_hbm, chain_ref),
        (att_bias_hbm, att_bias_own_ref),
        (chain_bias_hbm, chain_bias_ref),
        (out_hbm, out_ref),
        (mult_in_hbm, mult_in_ref),
        (mult_gate_hbm, mult_gate_ref),
        (mult_out_hbm, mult_out_ref),
        (trans_up_hbm, trans_up_ref),
        (trans_down_hbm, trans_down_ref),
    )
    copies = [
        pltpu.make_async_copy(src, dst, copy_sems.at[at]) for at, (src, dst) in enumerate(pairs)
    ]
    for copy in copies:
        copy.start()
    rows, cols, width = own_ref.shape
    heads = plain_bias_ref.shape[0]
    total = plain_bias_ref.shape[1]
    col_index = lax.axis_index("col")
    normed_ref[:, total:, :] = jnp.zeros((rows, WIDE - total, width), F32)
    att_bias_ref[...] = jnp.zeros(att_bias_ref.shape, F32)
    for copy in copies[:6]:
        copy.wait()
    for ref, col in ((own_ref, col_index), (near_ref, 1 - col_index)):
        value = ref[...].astype(F32)
        at = pl.ds(pl.multiple_of(col * cols, 8), cols)
        raw_ref[:, at, :] = value
        normed_ref[:, at, :] = norm(value)
    for part, at in ((1, None), (0, 0), (2, 1), (3, 2)):
        both = jnp.concatenate([proj_ref[part], proj_other_ref[part]], axis=0)
        if at is None:
            key_weights_ref[...] = both
        else:
            turned_weights_ref[at * width : (at + 1) * width] = both
    out_weights_ref[...] = jnp.concatenate([out_ref[...], out_other_ref[...]], axis=0)
    att_bias_ref[0 : heads // 2] = att_bias_own_ref[...].astype(F32)
    att_bias_ref[heads // 2 : heads] = att_bias_other_ref[...].astype(F32)
    length = length_ref[0]
    side = 2 * WIDE
    chain = chain_ref[...].astype(F32)
    chain = jnp.concatenate([chain, jnp.zeros((1, side - total), F32)], axis=1)
    chain = jnp.broadcast_to(chain, (side, side))
    same = (chain == chain.T).astype(F32)[:total]
    place = lax.broadcasted_iota(jnp.int32, (total, side), 1)
    masked = jnp.where(place < length, 0.0, -1000000000.0)
    for head in range(heads):
        from_ref = chain_bias_ref if head < heads // 2 else chain_bias_other_ref
        at = head % (heads // 2)
        plain_bias_ref[head, :, :] = from_ref[:, at : at + 1] * same + masked
    down = lax.broadcasted_iota(jnp.int32, (total, width), 0)
    valid_ref[...] = (down < length).astype(F32)
    tokens = [flat_pair(normed_ref, 2 * at).astype(BF16) for at in range(rows // 2)]
    weights = att_bias_ref[...].astype(BF16)
    for at in range(rows // 2):
        bias_rows(weights, tokens[at], turn_ref, 2 * at)
    scores, values, gates = project(
        tokens, turned_weights_ref[...], key_weights_ref[...], heads, total
    )
    for at in range(rows // 2):
        scores_ref[at] = scores[at]
        values_ref[at] = values[at]
        gates_ref[at] = gates[at]
    for copy in copies[6:]:
        copy.wait()


def finish(
    *refs,
    sources,
):
    count = len(sources)
    block_refs = refs[:count]
    (
        turned_weights_ref,
        key_weights_ref,
        out_weights_ref,
        att_bias_ref,
        plain_bias_ref,
        valid_ref,
        raw_own_ref,
        normed_own_ref,
        scores_ref,
        values_ref,
        gates_ref,
        turn_own_ref,
        mult_in_ref,
        mult_gate_ref,
        mult_out_ref,
        trans_up_ref,
        trans_down_ref,
        result_ref,
        normed_ref,
        raw_ref,
        turn_ref,
        bias_ref,
        left_ref,
        right_ref,
        first_ref,
        tile_ref,
    ) = refs[count:]
    rows, cols, width = block_refs[0].shape
    total = normed_ref.shape[0]
    heads = plain_bias_ref.shape[0]
    head_dim = width // heads
    row_index = lax.axis_index("row")
    col_index = lax.axis_index("col")
    sub_index = lax.axis_index("sub")
    other_rows = col_index * lax.axis_size("sub") + sub_index
    side = 2 * WIDE

    normed_ref[:, total:, :] = jnp.zeros((total, WIDE - total, width), F32)
    for ref, (row_step, col_step) in zip(block_refs, sources):
        row_off = jnp.where(sub_index == 0, row_step[0], row_step[1])
        col_off = jnp.where(sub_index == 0, col_step[0], col_step[1])
        value = ref[...].astype(F32)
        down = pl.ds((row_index ^ row_off) * rows, rows)
        along = pl.ds(pl.multiple_of((col_index ^ col_off) * cols, 8), cols)
        raw_ref[down, along, :] = value
        normed_ref[down, along, :] = norm(value)
    own_rows = pl.ds(row_index * rows, rows)
    weights = att_bias_ref[...].astype(BF16)
    for step in range(1, total // rows):
        start = (row_index ^ step) * rows
        for at in range(rows // 2):
            tokens = flat_pair(normed_ref, start + 2 * at).astype(BF16)
            bias_rows(weights, tokens, turn_ref, start + 2 * at)
    turn_ref[own_rows] = turn_own_ref[...]
    for head in range(heads):
        value = turn_ref[:, head, :] + plain_bias_ref[head]
        value = jnp.concatenate([value, jnp.zeros((WIDE - total, side), F32)], axis=0)
        value = jnp.concatenate([value, value], axis=0).T
        bias_ref[pl.ds(head * total, total)] = value[:total]

    first_lanes, second_lanes = lane_masks()
    pad = jnp.zeros((WIDE - total, side), BF16)
    out_weights = out_weights_ref[...]

    def attend(scores, values, gates):
        weights = []
        for head in range(heads):
            at = slice(head * total, (head + 1) * total)
            bias = bias_ref[at]
            parts = [score[at] + bias for score in scores]
            parts = [jnp.exp(part - jnp.max(part, axis=0, keepdims=True)) for part in parts]
            weights.append(
                [(part / jnp.sum(part, axis=0, keepdims=True)).astype(BF16) for part in parts]
            )
        attended = []
        for at in range(len(scores)):
            parts = []
            for head in range(heads):
                each = weights[head][at]
                spread_weights = jnp.concatenate(
                    [each * first_lanes, pad, each * second_lanes, pad], axis=0
                )
                parts.append(
                    dot(values[at][head * head_dim : (head + 1) * head_dim], spread_weights)
                )
            attended.append((jnp.concatenate(parts, axis=0) * gates[at]).astype(BF16))
        return [dot(each, out_weights, TN) for each in attended]

    def halves(firsts, starts, column):
        mixed = [norm(first).astype(BF16) for first in firsts]
        boths = [dot(each, mult_in_ref[:, column : column + 2 * width]) for each in mixed]
        values = [jax.nn.sigmoid(both[:, width:]) * both[:, :width] for both in boths]
        results = []
        for value, start in zip(values, starts):
            for which in range(2):
                row_valid = valid_ref[pl.ds(start + which, 1), :]
                each = value[which * WIDE : which * WIDE + total] * (valid_ref[...] * row_valid)
                results.append(each.astype(BF16).astype(F32))
        return results

    steps = range(rows // 2)
    start = other_rows * rows

    @pl.when(other_rows == row_index)
    def _():
        raw_ref[own_rows] = raw_own_ref[...]
        normed_ref[own_rows] = normed_own_ref[...]

    tokens = [flat_pair(normed_ref, start + 2 * at).astype(BF16) for at in steps]
    scores, values, gates = project(
        tokens, turned_weights_ref[...], key_weights_ref[...], heads, total
    )
    def run(own, group):
        if own:
            updates = attend(
                [scores_ref[at] for at in group],
                [values_ref[at] for at in group],
                [gates_ref[at] for at in group],
            )
            raws = [flat_pair(raw_own_ref, 2 * at) for at in group]
            starts = [row_index * rows + 2 * at for at in group]
        else:
            updates = attend(
                [scores[at] for at in group],
                [values[at] for at in group],
                [gates[at] for at in group],
            )
            starts = [start + 2 * at for at in group]
            raws = [flat_pair(raw_ref, at) for at in starts]
        firsts = [raw + update for raw, update in zip(raws, updates)]
        if own:
            for at, first in zip(group, firsts):
                first_ref[2 * at : 2 * at + 2] = first.reshape(2, WIDE, width)
        results = halves(firsts, starts, 0 if own else 2 * width)
        into_ref = left_ref if own else right_ref
        for at, each in enumerate(results):
            into_ref[2 * group[0] + at] = each

    for own in (True, False):
        for at in range(0, rows // 2, GROUP):
            run(own, list(range(at, at + GROUP)))

    half = rows
    for block in range(total // half):

        @pl.when(other_rows == block)
        def _():
            tile_ref[:, :half, :] = first_ref[:, block * half : (block + 1) * half, :]

    def triangle(step, carry):
        left = left_ref[step]
        sums = [
            jnp.sum(left * right_ref[other], axis=0, keepdims=True) for other in range(half)
        ]
        first_ref[step, :half, :] = jnp.concatenate(sums, axis=0)
        return carry

    lax.fori_loop(0, rows, triangle, 0)
    deep = tile_ref.shape[1]
    first = tile_ref[...].reshape(rows * deep, width)
    tri = first_ref[:, :deep, :].reshape(rows * deep, width)
    mixed = norm(first).astype(BF16)
    gate = jax.nn.sigmoid(dot(mixed, mult_gate_ref[...]))
    second = first + gate * dot(norm(tri).astype(BF16), mult_out_ref[...])
    hidden = jax.nn.relu(dot(norm(second).astype(BF16), trans_up_ref[...])).astype(BF16)
    result = second + dot(hidden, trans_down_ref[...])
    result_ref[...] = result.astype(BF16).reshape(rows, deep, width)[:, :half, :]


def gathered(
    pair,
    length,
    chain,
    att_proj,
    att_bias,
    chain_bias,
    att_out,
    mult_in,
    mult_gate,
    mult_out,
    trans_up,
    trans_down,
):
    rows, cols, width = pair.shape
    row_count = lax.axis_size("row")
    col_count = lax.axis_size("col")
    sub_count = lax.axis_size("sub")
    total = rows * row_count
    heads = att_bias.shape[1] * sub_count
    axes = ("row", "col", "sub")
    side = 2 * WIDE

    def place(row, col, sub):
        return (row * col_count + col) * sub_count + sub

    def exchange(value, offsets):
        routes = [
            (place(row, col, sub), place(row ^ offsets[sub][0], col ^ offsets[sub][1], sub))
            for row in range(row_count)
            for col in range(col_count)
            for sub in range(sub_count)
        ]
        return lax.ppermute(value, axes, routes)

    swap = functools.partial(lax.ppermute, axis_name="sub", perm=[(0, 1), (1, 0)])
    near = exchange(pair, STEPS[0])
    fetched = [exchange(pair, offsets) for offsets in STEPS[1:]]
    proj_other = swap(att_proj)
    out_other = swap(att_out)
    bias_other = swap(att_bias)
    chain_other = swap(chain_bias)
    blocks, sources = [], []
    for value, offsets in zip(fetched, STEPS[1:]):
        mine = tuple(zip(offsets[0], offsets[1]))
        blocks.append(value)
        sources.append(mine)
        if offsets[0] != offsets[1]:
            blocks.append(swap(value))
            sources.append(tuple((b, a) for a, b in mine))
    smem = pl.BlockSpec(memory_space=pltpu.SMEM)
    vmem = pl.BlockSpec(memory_space=pltpu.VMEM)
    hbm = pl.BlockSpec(memory_space=pltpu.HBM)
    params = [
        chain.reshape(1, total),
        pair,
        att_proj.transpose(1, 2, 0),
        att_bias.T,
        chain_bias.reshape(1, -1),
        att_out,
        mult_in,
        mult_gate,
        mult_out,
        trans_up,
        trans_down,
    ]
    params = [pltpu.with_memory_space_constraint(each, pltpu.HBM) for each in params]
    early = [
        near,
        proj_other.transpose(1, 2, 0),
        bias_other.T,
        chain_other.reshape(1, -1),
        out_other,
    ]
    shape = jax.ShapeDtypeStruct
    scratch = lambda each: pltpu.VMEM(each.shape, each.dtype)
    ready = pl.pallas_call(
        prepare,
        out_shape=[
            shape((3 * width, width), BF16),
            shape((width, width), BF16),
            shape((width, width), BF16),
            shape((8, width), F32),
            shape((heads, total, side), F32),
            shape((total, width), F32),
            shape((rows, WIDE, width), F32),
            shape((rows, WIDE, width), F32),
            shape((rows // 2, heads * total, side), F32),
            shape((rows // 2, width, side), BF16),
            shape((rows // 2, width, side), F32),
            shape((rows, 8, side), F32),
            *[shape(each.shape, each.dtype) for each in params[-5:]],
        ],
        in_specs=[smem] + [hbm] * len(params) + [vmem] * len(early),
        out_specs=[vmem] * 17,
        scratch_shapes=[
            scratch(params[0]),
            scratch(params[1]),
            scratch(params[2]),
            scratch(params[3]),
            scratch(params[4]),
            scratch(params[5]),
            pltpu.SemaphoreType.DMA((len(params),)),
        ],
        compiler_params=pltpu.CompilerParams(vmem_limit_bytes=LIMIT),
    )(length, *params, *early)
    operands = [*blocks, *ready]
    deep = 16
    return pl.pallas_call(
        functools.partial(finish, sources=tuple(sources)),
        out_shape=shape((rows, cols // sub_count, width), BF16),
        in_specs=[vmem] * len(operands),
        out_specs=vmem,
        scratch_shapes=[
            pltpu.VMEM((total, WIDE, width), F32),
            pltpu.VMEM((total, WIDE, width), F32),
            pltpu.VMEM((total, 8, side), F32),
            pltpu.VMEM((heads * total, side), F32),
            pltpu.VMEM((rows, total, width), F32),
            pltpu.VMEM((rows, total, width), F32),
            pltpu.VMEM((rows, WIDE, width), F32),
            pltpu.VMEM((rows, deep, width), F32),
        ],
        compiler_params=pltpu.CompilerParams(vmem_limit_bytes=LIMIT),
    )(*operands)


def solution(mesh):
    placed = (
        P(("grp", "row"), "col", None),
        P("grp"),
        P("grp"),
        P(None, None, "sub"),
        P(None, "sub"),
        P("sub"),
        P("sub", None),
        P(),
        P(),
        P(),
        P(),
        P(),
    )
    fits = replicated(mesh)
    return jax.shard_map(
        gathered if fits else local,
        mesh=mesh,
        in_specs=placed,
        out_specs=P(("grp", "row"), ("col", "sub"), None),
        check_vma=False,
    )
```

```python
import functools

import jax
import jax.numpy as jnp
from jax import lax
from jax.experimental import pallas as pl
from jax.experimental.pallas import tpu as pltpu
from jax.sharding import PartitionSpec as P


def norm(value):
    mean = jnp.mean(value, axis=-1, keepdims=True)
    centred = value - mean
    variance = jnp.mean(centred * centred, axis=-1, keepdims=True)
    return centred * lax.rsqrt(variance + 1e-05)


def local(
    pair,
    length,
    chain,
    att_proj,
    att_bias,
    chain_bias,
    att_out,
    mult_in,
    mult_gate,
    mult_out,
    trans_up,
    trans_down,
):
    rows, cols, width = pair.shape
    row_count = lax.axis_size("row")
    sub_count = lax.axis_size("sub")
    row_index = lax.axis_index("row")
    col_index = lax.axis_index("col")
    sub_index = lax.axis_index("sub")
    total = rows * row_count
    half = cols // sub_count
    heads_here = att_bias.shape[1]
    spread = att_out.shape[0]
    head_dim = spread // heads_here
    mult_width = mult_out.shape[0]
    valid = (jnp.arange(total) < length[0]).astype(jnp.float32)
    normed = norm(pair.astype(jnp.float32)).astype(jnp.bfloat16)
    flat = normed.reshape(rows * cols, width)
    projected = jnp.dot(
        flat, att_proj.reshape(width, 4 * spread), preferred_element_type=jnp.float32
    ).reshape(rows, cols, 4, spread)
    query = (projected[:, :, 0] * head_dim ** (-0.5)).astype(jnp.bfloat16)
    keys = projected[:, :, 1].astype(jnp.bfloat16)
    values = projected[:, :, 2].astype(jnp.bfloat16)
    gating = jax.nn.sigmoid(projected[:, :, 3])
    bias_local = (
        jnp.dot(flat, att_bias, preferred_element_type=jnp.float32)
        .reshape(rows, cols, heads_here)
        .transpose(2, 0, 1)
    )
    keys_all, values_all = (
        lax.all_gather(keys, "col", axis=1, tiled=True),
        lax.all_gather(values, "col", axis=1, tiled=True),
    )
    column_bias = lax.all_gather(bias_local, "row", axis=1, tiled=True)
    bias_here = lax.all_to_all(column_bias, "col", split_axis=1, concat_axis=2, tiled=True)
    chain_here = lax.dynamic_slice_in_dim(chain, col_index * cols, cols, 0)
    same = (chain_here[:, None] == chain[None, :]).astype(jnp.float32)
    bias_here = (
        bias_here
        + chain_bias[:, None, None] * same[None]
        + (valid[None, None, :] - 1.0) * 1000000000.0
    )

    def attend(block):
        block_query, block_keys, block_values = block
        scores = (
            jnp.einsum(
                "ajhd,akhd->ahjk", block_query, block_keys, preferred_element_type=jnp.float32
            )
            + bias_here[None]
        )
        weights = jax.nn.softmax(scores, axis=-1).astype(jnp.bfloat16)
        return jnp.einsum(
            "ahjk,akhd->ajhd", weights, block_values, preferred_element_type=jnp.float32
        )

    attended = lax.map(
        attend,
        (
            query.reshape(rows // 2, 2, cols, heads_here, head_dim),
            keys_all.reshape(rows // 2, 2, total, heads_here, head_dim),
            values_all.reshape(rows // 2, 2, total, heads_here, head_dim),
        ),
    )
    attended = (attended.reshape(rows, cols, spread) * gating).astype(jnp.bfloat16)
    update = jnp.dot(
        attended.reshape(rows * cols, spread), att_out, preferred_element_type=jnp.float32
    ).reshape(rows, cols, width)
    update_half = lax.psum_scatter(
        update.astype(jnp.bfloat16), "sub", scatter_dimension=1, tiled=True
    ).astype(jnp.float32)
    pair_half = lax.dynamic_slice_in_dim(pair, sub_index * half, half, 1).astype(jnp.float32)
    first = pair_half + update_half
    mixed = norm(first).astype(jnp.bfloat16)
    mixed_flat = mixed.reshape(rows * half, width)
    quad = jnp.dot(mixed_flat, mult_in, preferred_element_type=jnp.float32).reshape(
        rows, half, 4, mult_width
    )
    row_valid = lax.dynamic_slice_in_dim(valid, row_index * rows, rows, 0)
    col_valid = lax.dynamic_slice_in_dim(valid, col_index * cols + sub_index * half, half, 0)
    outer = row_valid[:, None, None] * col_valid[None, :, None]
    left = (outer * jax.nn.sigmoid(quad[:, :, 1]) * quad[:, :, 0]).astype(jnp.bfloat16)
    right = (outer * jax.nn.sigmoid(quad[:, :, 3]) * quad[:, :, 2]).astype(jnp.bfloat16)
    gate_out = jax.nn.sigmoid(jnp.dot(mixed_flat, mult_gate, preferred_element_type=jnp.float32))
    partial_value = jnp.einsum(
        "ikc,jkc->ijc",
        left,
        lax.all_gather(right, "row", axis=0, tiled=True),
        preferred_element_type=jnp.float32,
    )
    tri = lax.psum_scatter(
        partial_value.astype(jnp.bfloat16), ("col", "sub"), scatter_dimension=1, tiled=True
    ).astype(jnp.float32)
    tri_normed = norm(tri).astype(jnp.bfloat16).reshape(rows * half, mult_width)
    second = first + (
        gate_out * jnp.dot(tri_normed, mult_out, preferred_element_type=jnp.float32)
    ).reshape(rows, half, width)
    last_normed = norm(second).astype(jnp.bfloat16).reshape(rows * half, width)
    hidden = jax.nn.relu(jnp.dot(last_normed, trans_up, preferred_element_type=jnp.float32)).astype(
        jnp.bfloat16
    )
    result = second + jnp.dot(hidden, trans_down, preferred_element_type=jnp.float32).reshape(
        rows, half, width
    )
    return result.astype(jnp.bfloat16)


NT = (((1,), (1,)), ((), ()))
TN = (((0,), (0,)), ((), ()))
F32 = jnp.float32
BF16 = jnp.bfloat16
WIDE = 64
GROUP = 6
LIMIT = 16 * 1024 * 1024
STEPS = (((0, 1), (0, 1)), ((3, 1), (2, 1)), ((3, 0), (1, 0)), ((1, 1), (2, 0)))


def replicated(mesh):
    shape = mesh.shape
    return shape["row"] == 4 and shape["col"] == 2 and shape["sub"] == 2


def dot(left, right, dims=(((1,), (0,)), ((), ()))):
    return lax.dot_general(left, right, dims, preferred_element_type=F32)


def flat_pair(ref, start):
    return ref[pl.ds(start, 2)].reshape(2 * ref.shape[1], ref.shape[2])


def head_masks(heads, width):
    channel = lax.broadcasted_iota(jnp.int32, (1, width), 1)
    size = width // heads
    return [
        ((channel >= head * size) & (channel < (head + 1) * size)).astype(BF16)
        for head in range(heads)
    ]


def lane_masks():
    lane = lax.broadcasted_iota(jnp.int32, (1, 2 * WIDE), 1)
    return (lane < WIDE).astype(BF16), (lane >= WIDE).astype(BF16)


def project(tokens, turned_weights, key_weights, heads, total):
    width = tokens[0].shape[1]
    first_lanes, second_lanes = lane_masks()
    masks = head_masks(heads, width)
    turned = [dot(turned_weights, flat, NT) for flat in tokens]
    keys = [dot(flat, key_weights, NT).astype(BF16) for flat in tokens]
    scores = []
    for key, turn in zip(keys, turned):
        query = (turn[:width] * (width // heads) ** (-0.5)).astype(BF16)
        spread_keys = jnp.concatenate(
            [
                jnp.concatenate([key[at : at + total] * mask for mask in masks], axis=0)
                for at in (0, WIDE)
            ],
            axis=1,
        )
        spread_query = jnp.concatenate([query * first_lanes, query * second_lanes], axis=0)
        scores.append(dot(spread_keys, spread_query))
    values = [turn[width : 2 * width].astype(BF16) for turn in turned]
    gates = [jax.nn.sigmoid(turn[2 * width :]) for turn in turned]
    return scores, values, gates


def block_norm(ref):
    block = ref[...]
    flat = block.reshape(-1, block.shape[-1])
    ones = jnp.full((block.shape[-1], block.shape[-1]), 1.0 / block.shape[-1], BF16)
    value = flat.astype(F32)
    centred = value - dot(flat, ones)
    variance = jnp.mean(centred * centred, axis=-1, keepdims=True)
    result = centred * lax.rsqrt(variance + 1e-05)
    return value.reshape(block.shape), result.reshape(block.shape)


def bias_rows(weights, tokens, turn_ref, row):
    both = dot(weights, tokens, NT)
    turn_ref[row] = both
    turn_ref[row + 1] = pltpu.roll(both, WIDE, 1)


def prepare(
    length_ref,
    chain_hbm,
    own_hbm,
    proj_hbm,
    att_bias_hbm,
    chain_bias_hbm,
    out_hbm,
    mult_in_hbm,
    mult_gate_hbm,
    mult_out_hbm,
    trans_up_hbm,
    trans_down_hbm,
    near_ref,
    proj_other_ref,
    att_bias_other_ref,
    chain_bias_other_ref,
    out_other_ref,
    turned_weights_ref,
    key_weights_ref,
    out_weights_ref,
    att_bias_ref,
    plain_bias_ref,
    valid_ref,
    raw_ref,
    normed_ref,
    scores_ref,
    values_ref,
    gates_ref,
    turn_ref,
    mult_in_ref,
    mult_gate_ref,
    mult_out_ref,
    trans_up_ref,
    trans_down_ref,
    chain_ref,
    own_ref,
    proj_ref,
    att_bias_own_ref,
    chain_bias_ref,
    out_ref,
    copy_sems,
):
    pairs = (
        (own_hbm, own_ref),
        (proj_hbm, proj_ref),
        (chain_hbm, chain_ref),
        (att_bias_hbm, att_bias_own_ref),
        (chain_bias_hbm, chain_bias_ref),
        (out_hbm, out_ref),
        (mult_in_hbm, mult_in_ref),
        (mult_gate_hbm, mult_gate_ref),
        (mult_out_hbm, mult_out_ref),
        (trans_up_hbm, trans_up_ref),
        (trans_down_hbm, trans_down_ref),
    )
    copies = [
        pltpu.make_async_copy(src, dst, copy_sems.at[at]) for at, (src, dst) in enumerate(pairs)
    ]
    for copy in copies:
        copy.start()
    rows, cols, width = own_ref.shape
    heads = plain_bias_ref.shape[0]
    total = plain_bias_ref.shape[1]
    col_index = lax.axis_index("col")
    normed_ref[:, total:, :] = jnp.zeros((rows, WIDE - total, width), F32)
    att_bias_ref[...] = jnp.zeros(att_bias_ref.shape, F32)
    for copy in copies[:6]:
        copy.wait()
    for ref, col in ((own_ref, col_index), (near_ref, 1 - col_index)):
        at = pl.ds(pl.multiple_of(col * cols, 8), cols)
        value, result = block_norm(ref)
        raw_ref[:, at, :] = value
        normed_ref[:, at, :] = result
    for part, at in ((1, None), (0, 0), (2, 1), (3, 2)):
        both = jnp.concatenate([proj_ref[part], proj_other_ref[part]], axis=0)
        if at is None:
            key_weights_ref[...] = both
        else:
            turned_weights_ref[at * width : (at + 1) * width] = both
    out_weights_ref[...] = jnp.concatenate([out_ref[...], out_other_ref[...]], axis=0)
    att_bias_ref[0 : heads // 2] = att_bias_own_ref[...].astype(F32)
    att_bias_ref[heads // 2 : heads] = att_bias_other_ref[...].astype(F32)
    length = length_ref[0]
    side = 2 * WIDE
    chain = chain_ref[...].astype(F32)
    chain = jnp.concatenate([chain, jnp.zeros((1, side - total), F32)], axis=1)
    chain = jnp.broadcast_to(chain, (side, side))
    same = (chain == chain.T).astype(F32)[:total]
    place = lax.broadcasted_iota(jnp.int32, (total, side), 1)
    masked = jnp.where(place < length, 0.0, -1000000000.0)
    for head in range(heads):
        from_ref = chain_bias_ref if head < heads // 2 else chain_bias_other_ref
        at = head % (heads // 2)
        plain_bias_ref[head, :, :] = from_ref[:, at : at + 1] * same + masked
    down = lax.broadcasted_iota(jnp.int32, (total, width), 0)
    valid_ref[...] = (down < length).astype(F32)
    tokens = [flat_pair(normed_ref, 2 * at).astype(BF16) for at in range(rows // 2)]
    weights = att_bias_ref[...].astype(BF16)
    for at in range(rows // 2):
        bias_rows(weights, tokens[at], turn_ref, 2 * at)
    scores, values, gates = project(
        tokens, turned_weights_ref[...], key_weights_ref[...], heads, total
    )
    for at in range(rows // 2):
        scores_ref[at] = scores[at]
        values_ref[at] = values[at]
        gates_ref[at] = gates[at]
    for copy in copies[6:]:
        copy.wait()


def scatter(block_refs, sources, raw_ref, normed_ref):
    sub_index = lax.axis_index("sub")
    for ref, (row_step, col_step) in zip(block_refs, sources):
        rows, cols, _ = ref.shape
        row_block = lax.axis_index("row") ^ jnp.where(sub_index == 0, *row_step)
        col_block = lax.axis_index("col") ^ jnp.where(sub_index == 0, *col_step)
        down = pl.ds(row_block * rows, rows)
        along = pl.ds(pl.multiple_of(col_block * cols, 8), cols)
        value, result = block_norm(ref)
        raw_ref[down, along, :] = value
        normed_ref[down, along, :] = result


def whole_rows(att_bias_ref, normed_ref, turn_ref, rows, row_step):
    weights = att_bias_ref[...].astype(BF16)
    start = (lax.axis_index("row") ^ jnp.where(lax.axis_index("sub") == 0, *row_step)) * rows
    for at in range(rows // 2):
        tokens = flat_pair(normed_ref, start + 2 * at).astype(BF16)
        bias_rows(weights, tokens, turn_ref, start + 2 * at)


def collect(*refs, sources, row_steps, late_step):
    count = len(sources)
    (
        att_bias_ref,
        raw_own_ref,
        normed_own_ref,
        turn_own_ref,
        turn_ref,
        raw_other_ref,
        normed_other_ref,
        normed_late_ref,
        raw_ref,
        normed_ref,
    ) = refs[count:]
    total, wide, width = normed_ref.shape
    rows = raw_own_ref.shape[0]
    row_index = lax.axis_index("row")
    sub_index = lax.axis_index("sub")
    normed_ref[:, total:, :] = jnp.zeros((total, wide - total, width), F32)
    scatter(refs[:count], sources, raw_ref, normed_ref)
    own_rows = pl.ds(row_index * rows, rows)
    raw_ref[own_rows] = raw_own_ref[...]
    normed_ref[own_rows] = normed_own_ref[...]
    turn_ref[own_rows] = turn_own_ref[...]
    for row_step in row_steps:
        whole_rows(att_bias_ref, normed_ref, turn_ref, rows, row_step)
    other_rows = lax.axis_index("col") * lax.axis_size("sub") + sub_index
    late_rows = row_index ^ jnp.where(sub_index == 0, *late_step)
    raw_other_ref[...] = raw_ref[pl.ds(other_rows * rows, rows)]
    normed_other_ref[...] = normed_ref[pl.ds(other_rows * rows, rows)]
    normed_late_ref[...] = normed_ref[pl.ds(late_rows * rows, rows)]


def finish(*refs, source):
    (
        block_ref,
        turned_weights_ref,
        key_weights_ref,
        out_weights_ref,
        att_bias_ref,
        plain_bias_ref,
        valid_ref,
        raw_own_ref,
        _,
        scores_ref,
        values_ref,
        gates_ref,
        _,
        mult_in_ref,
        mult_gate_ref,
        mult_out_ref,
        trans_up_ref,
        trans_down_ref,
        turn_early_ref,
        raw_early_ref,
        normed_early_ref,
        late_early_ref,
        result_ref,
        raw_ref,
        normed_ref,
        late_ref,
        turn_ref,
        bias_ref,
        left_ref,
        right_ref,
        first_ref,
        tile_ref,
    ) = refs
    rows, cols, width = block_ref.shape
    total = valid_ref.shape[0]
    heads = plain_bias_ref.shape[0]
    head_dim = width // heads
    row_index = lax.axis_index("row")
    col_index = lax.axis_index("col")
    sub_index = lax.axis_index("sub")
    other_rows = col_index * lax.axis_size("sub") + sub_index
    side = 2 * WIDE

    row_step, col_step = source
    late_rows = row_index ^ jnp.where(sub_index == 0, *row_step)
    col_block = col_index ^ jnp.where(sub_index == 0, *col_step)
    along = pl.ds(pl.multiple_of(col_block * cols, 8), cols)
    value, result = block_norm(block_ref)
    late_ref[...] = late_early_ref[...]
    late_ref[:, along, :] = result
    turn_ref[...] = turn_early_ref[...]
    weights = att_bias_ref[...].astype(BF16)
    for at in range(rows // 2):
        tokens = flat_pair(late_ref, 2 * at).astype(BF16)
        bias_rows(weights, tokens, turn_ref, late_rows * rows + 2 * at)
    raw_ref[...] = raw_early_ref[...]
    normed_ref[...] = normed_early_ref[...]

    @pl.when(other_rows == late_rows)
    def _():
        raw_ref[:, along, :] = value
        normed_ref[:, along, :] = late_ref[:, along, :]

    for head in range(heads):
        value = turn_ref[:, head, :] + plain_bias_ref[head]
        value = jnp.concatenate([value, jnp.zeros((WIDE - total, side), F32)], axis=0)
        value = jnp.concatenate([value, value], axis=0).T
        bias_ref[pl.ds(head * total, total)] = value[:total]

    first_lanes, second_lanes = lane_masks()
    pad = jnp.zeros((WIDE - total, side), BF16)
    out_weights = out_weights_ref[...]

    def attend(scores, values, gates):
        weights = []
        for head in range(heads):
            at = slice(head * total, (head + 1) * total)
            bias = bias_ref[at]
            parts = [score[at] + bias for score in scores]
            parts = [jnp.exp(part - jnp.max(part, axis=0, keepdims=True)) for part in parts]
            weights.append(
                [(part / jnp.sum(part, axis=0, keepdims=True)).astype(BF16) for part in parts]
            )
        attended = []
        for at in range(len(scores)):
            parts = []
            for head in range(heads):
                each = weights[head][at]
                spread_weights = jnp.concatenate(
                    [each * first_lanes, pad, each * second_lanes, pad], axis=0
                )
                parts.append(
                    dot(values[at][head * head_dim : (head + 1) * head_dim], spread_weights)
                )
            attended.append((jnp.concatenate(parts, axis=0) * gates[at]).astype(BF16))
        return [dot(each, out_weights, TN) for each in attended]

    def halves(firsts, starts, column):
        mixed = [norm(first).astype(BF16) for first in firsts]
        boths = [dot(each, mult_in_ref[:, column : column + 2 * width]) for each in mixed]
        values = [jax.nn.sigmoid(both[:, width:]) * both[:, :width] for both in boths]
        results = []
        for value, start in zip(values, starts):
            for which in range(2):
                row_valid = valid_ref[pl.ds(start + which, 1), :]
                each = value[which * WIDE : which * WIDE + total] * (valid_ref[...] * row_valid)
                results.append(each.astype(BF16).astype(F32))
        return results

    steps = range(rows // 2)
    start = other_rows * rows

    tokens = [flat_pair(normed_ref, 2 * at).astype(BF16) for at in steps]
    scores, values, gates = project(
        tokens, turned_weights_ref[...], key_weights_ref[...], heads, total
    )

    def run(own, group):
        if own:
            updates = attend(
                [scores_ref[at] for at in group],
                [values_ref[at] for at in group],
                [gates_ref[at] for at in group],
            )
            raws = [flat_pair(raw_own_ref, 2 * at) for at in group]
            starts = [row_index * rows + 2 * at for at in group]
        else:
            updates = attend(
                [scores[at] for at in group],
                [values[at] for at in group],
                [gates[at] for at in group],
            )
            starts = [start + 2 * at for at in group]
            raws = [flat_pair(raw_ref, 2 * at) for at in group]
        firsts = [raw + update for raw, update in zip(raws, updates)]
        if own:
            for at, first in zip(group, firsts):
                first_ref[2 * at : 2 * at + 2] = first.reshape(2, WIDE, width)
        results = halves(firsts, starts, 0 if own else 2 * width)
        into_ref = left_ref if own else right_ref
        for at, each in enumerate(results):
            into_ref[2 * group[0] + at] = each

    for own in (True, False):
        for at in range(0, rows // 2, GROUP):
            run(own, list(range(at, at + GROUP)))

    half = rows
    for block in range(total // half):

        @pl.when(other_rows == block)
        def _():
            tile_ref[:, :half, :] = first_ref[:, block * half : (block + 1) * half, :]

    def triangle(step, carry):
        left = left_ref[step]
        sums = [
            jnp.sum(left * right_ref[other], axis=0, keepdims=True) for other in range(half)
        ]
        first_ref[step, :half, :] = jnp.concatenate(sums, axis=0)
        return carry

    lax.fori_loop(0, rows, triangle, 0)
    deep = tile_ref.shape[1]
    first = tile_ref[...].reshape(rows * deep, width)
    tri = first_ref[:, :deep, :].reshape(rows * deep, width)
    mixed = norm(first).astype(BF16)
    gate = jax.nn.sigmoid(dot(mixed, mult_gate_ref[...]))
    second = first + gate * dot(norm(tri).astype(BF16), mult_out_ref[...])
    hidden = jax.nn.relu(dot(norm(second).astype(BF16), trans_up_ref[...])).astype(BF16)
    result = second + dot(hidden, trans_down_ref[...])
    result_ref[...] = result.astype(BF16).reshape(rows, deep, width)[:, :half, :]


def gathered(
    pair,
    length,
    chain,
    att_proj,
    att_bias,
    chain_bias,
    att_out,
    mult_in,
    mult_gate,
    mult_out,
    trans_up,
    trans_down,
):
    rows, cols, width = pair.shape
    row_count = lax.axis_size("row")
    col_count = lax.axis_size("col")
    sub_count = lax.axis_size("sub")
    total = rows * row_count
    heads = att_bias.shape[1] * sub_count
    axes = ("row", "col", "sub")
    side = 2 * WIDE

    def place(row, col, sub):
        return (row * col_count + col) * sub_count + sub

    def exchange(value, offsets):
        routes = [
            (place(row, col, sub), place(row ^ offsets[sub][0], col ^ offsets[sub][1], sub))
            for row in range(row_count)
            for col in range(col_count)
            for sub in range(sub_count)
        ]
        return lax.ppermute(value, axes, routes)

    swap = functools.partial(lax.ppermute, axis_name="sub", perm=[(0, 1), (1, 0)])
    fetched = []
    for offsets in STEPS:
        fetched.append(exchange(pair, offsets))
    proj_other = swap(att_proj)
    out_other = swap(att_out)
    bias_other = swap(att_bias)
    chain_other = swap(chain_bias)
    blocks, sources = [], []
    for value, offsets in zip(fetched, STEPS):
        if offsets == ((0, 1), (0, 1)):
            near = value
            continue
        mine = tuple(zip(offsets[0], offsets[1]))
        blocks.append(value)
        sources.append(mine)
        if offsets[0] != offsets[1]:
            blocks.append(swap(value))
            sources.append(tuple((b, a) for a, b in mine))
    smem = pl.BlockSpec(memory_space=pltpu.SMEM)
    vmem = pl.BlockSpec(memory_space=pltpu.VMEM)
    hbm = pl.BlockSpec(memory_space=pltpu.HBM)
    params = [
        chain.reshape(1, total),
        pair,
        att_proj.transpose(1, 2, 0),
        att_bias.T,
        chain_bias.reshape(1, -1),
        att_out,
        mult_in,
        mult_gate,
        mult_out,
        trans_up,
        trans_down,
    ]
    params = [pltpu.with_memory_space_constraint(each, pltpu.HBM) for each in params]
    early = [
        near,
        proj_other.transpose(1, 2, 0),
        bias_other.T,
        chain_other.reshape(1, -1),
        out_other,
    ]
    shape = jax.ShapeDtypeStruct
    scratch = lambda each: pltpu.VMEM(each.shape, each.dtype)
    ready = pl.pallas_call(
        prepare,
        out_shape=[
            shape((3 * width, width), BF16),
            shape((width, width), BF16),
            shape((width, width), BF16),
            shape((8, width), F32),
            shape((heads, total, side), F32),
            shape((total, width), F32),
            shape((rows, WIDE, width), F32),
            shape((rows, WIDE, width), F32),
            shape((rows // 2, heads * total, side), F32),
            shape((rows // 2, width, side), BF16),
            shape((rows // 2, width, side), F32),
            shape((rows, 8, side), F32),
            *[shape(each.shape, each.dtype) for each in params[-5:]],
        ],
        in_specs=[smem] + [hbm] * len(params) + [vmem] * len(early),
        out_specs=[vmem] * 17,
        scratch_shapes=[
            scratch(params[0]),
            scratch(params[1]),
            scratch(params[2]),
            scratch(params[3]),
            scratch(params[4]),
            scratch(params[5]),
            pltpu.SemaphoreType.DMA((len(params),)),
        ],
        compiler_params=pltpu.CompilerParams(vmem_limit_bytes=LIMIT),
    )(length, *params, *early)
    last = sources[-1][0]
    others = [[step for step in range(1, row_count) if step != late] for late in last]
    merged = pl.pallas_call(
        functools.partial(
            collect, sources=tuple(sources[:-1]), row_steps=tuple(zip(*others)), late_step=last
        ),
        out_shape=[shape((total, 8, side), F32)] + [shape((rows, WIDE, width), F32)] * 3,
        in_specs=[vmem] * (len(blocks) + 3),
        out_specs=[vmem] * 4,
        scratch_shapes=[pltpu.VMEM((total, WIDE, width), F32)] * 2,
        compiler_params=pltpu.CompilerParams(vmem_limit_bytes=LIMIT),
    )(*blocks[:-1], ready[3], ready[6], ready[7], ready[11])
    operands = [blocks[-1], *ready, *merged]
    deep = 16
    return pl.pallas_call(
        functools.partial(finish, source=sources[-1]),
        out_shape=shape((rows, cols // sub_count, width), BF16),
        in_specs=[vmem] * len(operands),
        out_specs=vmem,
        scratch_shapes=[
            *[pltpu.VMEM((rows, WIDE, width), F32)] * 3,
            pltpu.VMEM((total, 8, side), F32),
            pltpu.VMEM((heads * total, side), F32),
            pltpu.VMEM((rows, total, width), F32),
            pltpu.VMEM((rows, total, width), F32),
            pltpu.VMEM((rows, WIDE, width), F32),
            pltpu.VMEM((rows, deep, width), F32),
        ],
        compiler_params=pltpu.CompilerParams(vmem_limit_bytes=LIMIT),
    )(*operands)


def solution(mesh):
    placed = (
        P(("grp", "row"), "col", None),
        P("grp"),
        P("grp"),
        P(None, None, "sub"),
        P(None, "sub"),
        P("sub"),
        P("sub", None),
        P(),
        P(),
        P(),
        P(),
        P(),
    )
    fits = replicated(mesh)
    return jax.shard_map(
        gathered if fits else local,
        mesh=mesh,
        in_specs=placed,
        out_specs=P(("grp", "row"), ("col", "sub"), None),
        check_vma=False,
    )
```

```python
import functools

import jax
import jax.numpy as jnp
from jax import lax
from jax.experimental import pallas as pl
from jax.experimental.pallas import tpu as pltpu
from jax.sharding import PartitionSpec as P


def norm(value):
    mean = jnp.mean(value, axis=-1, keepdims=True)
    centred = value - mean
    variance = jnp.mean(centred * centred, axis=-1, keepdims=True)
    return centred * lax.rsqrt(variance + 1e-05)


def local(
    pair,
    length,
    chain,
    att_proj,
    att_bias,
    chain_bias,
    att_out,
    mult_in,
    mult_gate,
    mult_out,
    trans_up,
    trans_down,
):
    rows, cols, width = pair.shape
    row_count = lax.axis_size("row")
    sub_count = lax.axis_size("sub")
    row_index = lax.axis_index("row")
    col_index = lax.axis_index("col")
    sub_index = lax.axis_index("sub")
    total = rows * row_count
    half = cols // sub_count
    heads_here = att_bias.shape[1]
    spread = att_out.shape[0]
    head_dim = spread // heads_here
    mult_width = mult_out.shape[0]
    valid = (jnp.arange(total) < length[0]).astype(jnp.float32)
    normed = norm(pair.astype(jnp.float32)).astype(jnp.bfloat16)
    flat = normed.reshape(rows * cols, width)
    projected = jnp.dot(
        flat, att_proj.reshape(width, 4 * spread), preferred_element_type=jnp.float32
    ).reshape(rows, cols, 4, spread)
    query = (projected[:, :, 0] * head_dim ** (-0.5)).astype(jnp.bfloat16)
    keys = projected[:, :, 1].astype(jnp.bfloat16)
    values = projected[:, :, 2].astype(jnp.bfloat16)
    gating = jax.nn.sigmoid(projected[:, :, 3])
    bias_local = (
        jnp.dot(flat, att_bias, preferred_element_type=jnp.float32)
        .reshape(rows, cols, heads_here)
        .transpose(2, 0, 1)
    )
    keys_all, values_all = (
        lax.all_gather(keys, "col", axis=1, tiled=True),
        lax.all_gather(values, "col", axis=1, tiled=True),
    )
    column_bias = lax.all_gather(bias_local, "row", axis=1, tiled=True)
    bias_here = lax.all_to_all(column_bias, "col", split_axis=1, concat_axis=2, tiled=True)
    chain_here = lax.dynamic_slice_in_dim(chain, col_index * cols, cols, 0)
    same = (chain_here[:, None] == chain[None, :]).astype(jnp.float32)
    bias_here = (
        bias_here
        + chain_bias[:, None, None] * same[None]
        + (valid[None, None, :] - 1.0) * 1000000000.0
    )

    def attend(block):
        block_query, block_keys, block_values = block
        scores = (
            jnp.einsum(
                "ajhd,akhd->ahjk", block_query, block_keys, preferred_element_type=jnp.float32
            )
            + bias_here[None]
        )
        weights = jax.nn.softmax(scores, axis=-1).astype(jnp.bfloat16)
        return jnp.einsum(
            "ahjk,akhd->ajhd", weights, block_values, preferred_element_type=jnp.float32
        )

    attended = lax.map(
        attend,
        (
            query.reshape(rows // 2, 2, cols, heads_here, head_dim),
            keys_all.reshape(rows // 2, 2, total, heads_here, head_dim),
            values_all.reshape(rows // 2, 2, total, heads_here, head_dim),
        ),
    )
    attended = (attended.reshape(rows, cols, spread) * gating).astype(jnp.bfloat16)
    update = jnp.dot(
        attended.reshape(rows * cols, spread), att_out, preferred_element_type=jnp.float32
    ).reshape(rows, cols, width)
    update_half = lax.psum_scatter(
        update.astype(jnp.bfloat16), "sub", scatter_dimension=1, tiled=True
    ).astype(jnp.float32)
    pair_half = lax.dynamic_slice_in_dim(pair, sub_index * half, half, 1).astype(jnp.float32)
    first = pair_half + update_half
    mixed = norm(first).astype(jnp.bfloat16)
    mixed_flat = mixed.reshape(rows * half, width)
    quad = jnp.dot(mixed_flat, mult_in, preferred_element_type=jnp.float32).reshape(
        rows, half, 4, mult_width
    )
    row_valid = lax.dynamic_slice_in_dim(valid, row_index * rows, rows, 0)
    col_valid = lax.dynamic_slice_in_dim(valid, col_index * cols + sub_index * half, half, 0)
    outer = row_valid[:, None, None] * col_valid[None, :, None]
    left = (outer * jax.nn.sigmoid(quad[:, :, 1]) * quad[:, :, 0]).astype(jnp.bfloat16)
    right = (outer * jax.nn.sigmoid(quad[:, :, 3]) * quad[:, :, 2]).astype(jnp.bfloat16)
    gate_out = jax.nn.sigmoid(jnp.dot(mixed_flat, mult_gate, preferred_element_type=jnp.float32))
    partial_value = jnp.einsum(
        "ikc,jkc->ijc",
        left,
        lax.all_gather(right, "row", axis=0, tiled=True),
        preferred_element_type=jnp.float32,
    )
    tri = lax.psum_scatter(
        partial_value.astype(jnp.bfloat16), ("col", "sub"), scatter_dimension=1, tiled=True
    ).astype(jnp.float32)
    tri_normed = norm(tri).astype(jnp.bfloat16).reshape(rows * half, mult_width)
    second = first + (
        gate_out * jnp.dot(tri_normed, mult_out, preferred_element_type=jnp.float32)
    ).reshape(rows, half, width)
    last_normed = norm(second).astype(jnp.bfloat16).reshape(rows * half, width)
    hidden = jax.nn.relu(jnp.dot(last_normed, trans_up, preferred_element_type=jnp.float32)).astype(
        jnp.bfloat16
    )
    result = second + jnp.dot(hidden, trans_down, preferred_element_type=jnp.float32).reshape(
        rows, half, width
    )
    return result.astype(jnp.bfloat16)


NT = (((1,), (1,)), ((), ()))
TN = (((0,), (0,)), ((), ()))
F32 = jnp.float32
BF16 = jnp.bfloat16
WIDE = 64
FLIP = True
GROUP = 6
LIMIT = 16 * 1024 * 1024
STEPS = (((0, 1), (0, 1)), ((3, 1), (2, 1)), ((3, 0), (1, 0)), ((1, 1), (2, 0)))


def moved(row, step, count, sign):
    return row ^ step if FLIP else lax.rem(row + count + sign * step, count)


def replicated(mesh):
    shape = mesh.shape
    return shape["row"] == 4 and shape["col"] == 2 and shape["sub"] == 2


def dot(left, right, dims=(((1,), (0,)), ((), ()))):
    return lax.dot_general(left, right, dims, preferred_element_type=F32)


def flat_pair(ref, start):
    return ref[pl.ds(start, 2)].reshape(2 * ref.shape[1], ref.shape[2])


def head_masks(heads, width):
    channel = lax.broadcasted_iota(jnp.int32, (1, width), 1)
    size = width // heads
    return [
        ((channel >= head * size) & (channel < (head + 1) * size)).astype(BF16)
        for head in range(heads)
    ]


def lane_masks():
    lane = lax.broadcasted_iota(jnp.int32, (1, 2 * WIDE), 1)
    return (lane < WIDE).astype(BF16), (lane >= WIDE).astype(BF16)


def project(tokens, turned_weights, key_weights, heads, total):
    width = tokens[0].shape[1]
    first_lanes, second_lanes = lane_masks()
    masks = head_masks(heads, width)
    turned = [dot(turned_weights, flat, NT) for flat in tokens]
    keys = [dot(flat, key_weights, NT).astype(BF16) for flat in tokens]
    scores = []
    for key, turn in zip(keys, turned):
        query = (turn[:width] * (width // heads) ** (-0.5)).astype(BF16)
        spread_keys = jnp.concatenate(
            [
                jnp.concatenate([key[at : at + total] * mask for mask in masks], axis=0)
                for at in (0, WIDE)
            ],
            axis=1,
        )
        spread_query = jnp.concatenate([query * first_lanes, query * second_lanes], axis=0)
        scores.append(dot(spread_keys, spread_query))
    values = [turn[width : 2 * width].astype(BF16) for turn in turned]
    gates = [jax.nn.sigmoid(turn[2 * width :]) for turn in turned]
    return scores, values, gates


def block_norm(ref):
    block = ref[...]
    flat = block.reshape(-1, block.shape[-1])
    ones = jnp.full((block.shape[-1], block.shape[-1]), 1.0 / block.shape[-1], BF16)
    value = flat.astype(F32)
    centred = value - dot(flat, ones)
    variance = jnp.mean(centred * centred, axis=-1, keepdims=True)
    result = centred * lax.rsqrt(variance + 1e-05)
    return value.reshape(block.shape), result.reshape(block.shape)


def split_norm(value):
    width = value.shape[-1]
    high = value.astype(BF16)
    low = (value - high.astype(F32)).astype(BF16)
    ones = jnp.full((2 * width, width), 1.0 / width, BF16)
    centred = value - dot(jnp.concatenate([high, low], axis=1), ones)
    variance = jnp.mean(centred * centred, axis=-1, keepdims=True)
    return centred * lax.rsqrt(variance + 1e-05)


def sum_down(parts):
    row = lax.broadcasted_iota(jnp.int32, parts[0].shape, 0)
    for distance in (1, 2, 4):
        keep = (row & distance) == 0
        parts = [
            jnp.where(keep, one, two) + pltpu.roll(jnp.where(keep, two, one), distance, 0)
            for one, two in zip(parts[0::2], parts[1::2])
        ]
    return parts[0]


def bias_rows(weights, tokens, turn_ref, row):
    both = dot(weights, tokens, NT)
    turn_ref[row] = both
    turn_ref[row + 1] = pltpu.roll(both, WIDE, 1)


def prepare(
    length_any,
    chain_hbm,
    own_hbm,
    proj_hbm,
    att_bias_hbm,
    chain_bias_hbm,
    out_hbm,
    mult_in_hbm,
    mult_gate_hbm,
    mult_out_hbm,
    trans_up_hbm,
    trans_down_hbm,
    near_ref,
    proj_other_ref,
    att_bias_other_ref,
    chain_bias_other_ref,
    out_other_ref,
    turned_weights_ref,
    key_weights_ref,
    out_weights_ref,
    att_bias_ref,
    plain_bias_ref,
    valid_ref,
    raw_ref,
    normed_ref,
    scores_ref,
    values_ref,
    gates_ref,
    turn_ref,
    mult_in_ref,
    mult_gate_ref,
    mult_out_ref,
    trans_up_ref,
    trans_down_ref,
    chain_ref,
    own_ref,
    proj_ref,
    att_bias_own_ref,
    chain_bias_ref,
    out_ref,
    length_ref,
    copy_sems,
):
    pairs = (
        (own_hbm, own_ref),
        (proj_hbm, proj_ref),
        (chain_hbm, chain_ref),
        (att_bias_hbm, att_bias_own_ref),
        (chain_bias_hbm, chain_bias_ref),
        (out_hbm, out_ref),
        (length_any, length_ref),
        (mult_in_hbm, mult_in_ref),
        (mult_gate_hbm, mult_gate_ref),
        (mult_out_hbm, mult_out_ref),
        (trans_up_hbm, trans_up_ref),
        (trans_down_hbm, trans_down_ref),
    )
    copies = [
        pltpu.make_async_copy(src, dst, copy_sems.at[at]) for at, (src, dst) in enumerate(pairs)
    ]
    for copy in copies:
        copy.start()
    rows, cols, width = own_ref.shape
    heads = plain_bias_ref.shape[0]
    total = plain_bias_ref.shape[1]
    col_index = lax.axis_index("col")
    normed_ref[:, total:, :] = jnp.zeros((rows, WIDE - total, width), F32)
    att_bias_ref[...] = jnp.zeros(att_bias_ref.shape, F32)
    for ref, col in ((near_ref, 1 - col_index), (own_ref, col_index)):
        if ref is own_ref:
            for copy in copies[:7]:
                copy.wait()
        at = pl.ds(pl.multiple_of(col * cols, 8), cols)
        value, result = block_norm(ref)
        raw_ref[:, at, :] = value
        normed_ref[:, at, :] = result
    for part, at in ((1, None), (0, 0), (2, 1), (3, 2)):
        both = jnp.concatenate([proj_ref[part], proj_other_ref[part]], axis=0)
        if at is None:
            key_weights_ref[...] = both
        else:
            turned_weights_ref[at * width : (at + 1) * width] = both
    out_weights_ref[...] = jnp.concatenate([out_ref[...], out_other_ref[...]], axis=0)
    att_bias_ref[0 : heads // 2] = att_bias_own_ref[...].astype(F32)
    att_bias_ref[heads // 2 : heads] = att_bias_other_ref[...].astype(F32)
    length = length_ref[0]
    side = 2 * WIDE
    chain = chain_ref[...].astype(F32)
    chain = jnp.concatenate([chain, jnp.zeros((1, side - total), F32)], axis=1)
    chain = jnp.broadcast_to(chain, (side, side))
    same = (chain == chain.T).astype(F32)[:total]
    place = lax.broadcasted_iota(jnp.int32, (total, side), 1)
    masked = jnp.where(place < length, 0.0, -1000000000.0)
    for head in range(heads):
        from_ref = chain_bias_ref if head < heads // 2 else chain_bias_other_ref
        at = head % (heads // 2)
        plain_bias_ref[head, :, :] = from_ref[:, at : at + 1] * same + masked
    down = lax.broadcasted_iota(jnp.int32, (total, width), 0)
    valid_ref[...] = (down < length).astype(F32)
    tokens = [flat_pair(normed_ref, 2 * at).astype(BF16) for at in range(rows // 2)]
    weights = att_bias_ref[...].astype(BF16)
    for at in range(rows // 2):
        bias_rows(weights, tokens[at], turn_ref, 2 * at)
    scores, values, gates = project(
        tokens, turned_weights_ref[...], key_weights_ref[...], heads, total
    )
    for at in range(rows // 2):
        scores_ref[at] = scores[at]
        values_ref[at] = values[at]
        gates_ref[at] = gates[at]
    for copy in copies[7:]:
        copy.wait()


def scatter(block_refs, sources, raw_ref, normed_ref):
    sub_index = lax.axis_index("sub")
    for ref, (row_step, col_step) in zip(block_refs, sources):
        rows, cols, _ = ref.shape
        row_block = moved(
            lax.axis_index("row"), jnp.where(sub_index == 0, *row_step), lax.axis_size("row"), -1
        )
        col_block = lax.axis_index("col") ^ jnp.where(sub_index == 0, *col_step)
        down = pl.ds(row_block * rows, rows)
        along = pl.ds(pl.multiple_of(col_block * cols, 8), cols)
        value, result = block_norm(ref)
        raw_ref[down, along, :] = value
        normed_ref[down, along, :] = result


def whole_rows(att_bias_ref, normed_ref, turn_ref, rows, row_step):
    weights = att_bias_ref[...].astype(BF16)
    start = moved(
        lax.axis_index("row"),
        jnp.where(lax.axis_index("sub") == 0, *row_step),
        lax.axis_size("row"),
        -1,
    )
    start = start * rows
    for at in range(rows // 2):
        tokens = flat_pair(normed_ref, start + 2 * at).astype(BF16)
        bias_rows(weights, tokens, turn_ref, start + 2 * at)


def collect(*refs, sources, row_steps, late_step):
    count = len(sources)
    (
        att_bias_ref,
        raw_own_ref,
        normed_own_ref,
        turn_own_ref,
        turn_ref,
        raw_other_ref,
        normed_other_ref,
        normed_late_ref,
        raw_ref,
        normed_ref,
    ) = refs[count:]
    total, wide, width = normed_ref.shape
    rows = raw_own_ref.shape[0]
    row_index = lax.axis_index("row")
    sub_index = lax.axis_index("sub")
    normed_ref[:, total:, :] = jnp.zeros((total, wide - total, width), F32)
    scatter(refs[:count], sources, raw_ref, normed_ref)
    own_rows = pl.ds(row_index * rows, rows)
    raw_ref[own_rows] = raw_own_ref[...]
    normed_ref[own_rows] = normed_own_ref[...]
    turn_ref[own_rows] = turn_own_ref[...]
    for row_step in row_steps:
        whole_rows(att_bias_ref, normed_ref, turn_ref, rows, row_step)
    other_rows = lax.axis_index("col") * lax.axis_size("sub") + sub_index
    late_rows = moved(
        row_index, jnp.where(sub_index == 0, *late_step), lax.axis_size("row"), -1
    )
    raw_other_ref[...] = raw_ref[pl.ds(other_rows * rows, rows)]
    normed_other_ref[...] = normed_ref[pl.ds(other_rows * rows, rows)]
    normed_late_ref[...] = normed_ref[pl.ds(late_rows * rows, rows)]


def finish(*refs, source):
    (
        block_ref,
        turned_weights_ref,
        key_weights_ref,
        out_weights_ref,
        att_bias_ref,
        plain_bias_ref,
        valid_ref,
        raw_own_ref,
        _,
        scores_ref,
        values_ref,
        gates_ref,
        _,
        mult_in_ref,
        mult_gate_ref,
        mult_out_ref,
        trans_up_ref,
        trans_down_ref,
        turn_early_ref,
        raw_early_ref,
        normed_early_ref,
        late_early_ref,
        result_ref,
        raw_ref,
        normed_ref,
        late_ref,
        turn_ref,
        bias_ref,
        left_ref,
        right_ref,
        first_ref,
        tile_ref,
        tri_ref,
    ) = refs
    rows, cols, width = block_ref.shape
    total = valid_ref.shape[0]
    heads = plain_bias_ref.shape[0]
    head_dim = width // heads
    row_index = lax.axis_index("row")
    col_index = lax.axis_index("col")
    sub_index = lax.axis_index("sub")
    other_rows = col_index * lax.axis_size("sub") + sub_index
    side = 2 * WIDE

    row_step, col_step = source
    late_rows = moved(
        row_index, jnp.where(sub_index == 0, *row_step), lax.axis_size("row"), -1
    )
    col_block = col_index ^ jnp.where(sub_index == 0, *col_step)
    along = pl.ds(pl.multiple_of(col_block * cols, 8), cols)
    value, result = block_norm(block_ref)
    late_ref[...] = late_early_ref[...]
    late_ref[:, along, :] = result
    turn_ref[...] = turn_early_ref[...]
    weights = att_bias_ref[...].astype(BF16)
    for at in range(rows // 2):
        tokens = flat_pair(late_ref, 2 * at).astype(BF16)
        bias_rows(weights, tokens, turn_ref, late_rows * rows + 2 * at)
    here = pl.ds(jnp.where(other_rows == late_rows, 0, rows), rows)
    raw_ref[:rows] = raw_early_ref[...]
    normed_ref[:rows] = normed_early_ref[...]
    raw_ref[here, along, :] = value
    normed_ref[here, along, :] = result

    for head in range(heads):
        value = turn_ref[:, head, :] + plain_bias_ref[head]
        value = jnp.concatenate([value, jnp.zeros((WIDE - total, side), F32)], axis=0)
        value = jnp.concatenate([value, value], axis=0).T
        bias_ref[pl.ds(head * total, total)] = value[:total]

    first_lanes, second_lanes = lane_masks()
    pad = jnp.zeros((WIDE - total, side), BF16)
    out_weights = out_weights_ref[...]

    def attend(scores, values, gates):
        weights = []
        for head in range(heads):
            at = slice(head * total, (head + 1) * total)
            bias = bias_ref[at]
            parts = [score[at] + bias for score in scores]
            parts = [jnp.exp(part - jnp.max(part, axis=0, keepdims=True)) for part in parts]
            weights.append(
                [(part / jnp.sum(part, axis=0, keepdims=True)).astype(BF16) for part in parts]
            )
        attended = []
        for at in range(len(scores)):
            parts = []
            for head in range(heads):
                each = weights[head][at]
                spread_weights = jnp.concatenate(
                    [each * first_lanes, pad, each * second_lanes, pad], axis=0
                )
                parts.append(
                    dot(values[at][head * head_dim : (head + 1) * head_dim], spread_weights)
                )
            attended.append((jnp.concatenate(parts, axis=0) * gates[at]).astype(BF16))
        updates = [dot(each, out_weights, TN) for each in attended]
        return [
            jnp.concatenate([each[:total], each[WIDE : WIDE + total]], axis=0) for each in updates
        ]

    def halves(firsts, starts, column):
        mixed = [split_norm(first).astype(BF16) for first in firsts]
        boths = [dot(each, mult_in_ref[:, column : column + 2 * width]) for each in mixed]
        values = [jax.nn.sigmoid(both[:, width:]) * both[:, :width] for both in boths]
        results = []
        for value, start in zip(values, starts):
            for which in range(2):
                row_valid = valid_ref[pl.ds(start + which, 1), :]
                each = value[which * total : (which + 1) * total] * (valid_ref[...] * row_valid)
                results.append(each.astype(BF16).astype(F32))
        return results

    steps = range(rows // 2)
    start = other_rows * rows

    tokens = [flat_pair(normed_ref, 2 * at).astype(BF16) for at in steps]
    scores, values, gates = project(
        tokens, turned_weights_ref[...], key_weights_ref[...], heads, total
    )

    def run(own, group):
        if own:
            updates = attend(
                [scores_ref[at] for at in group],
                [values_ref[at] for at in group],
                [gates_ref[at] for at in group],
            )
            raws = [raw_own_ref[2 * at : 2 * at + 2, :total, :] for at in group]
            starts = [row_index * rows + 2 * at for at in group]
        else:
            updates = attend(
                [scores[at] for at in group],
                [values[at] for at in group],
                [gates[at] for at in group],
            )
            starts = [start + 2 * at for at in group]
            raws = [raw_ref[2 * at : 2 * at + 2, :total, :] for at in group]
        firsts = [raw.reshape(2 * total, width) + update for raw, update in zip(raws, updates)]
        if own:
            for at, first in zip(group, firsts):
                first_ref[2 * at : 2 * at + 2] = first.reshape(2, total, width)
        results = halves(firsts, starts, 0 if own else 2 * width)
        into_ref = left_ref if own else right_ref
        for at, each in enumerate(results):
            into_ref[2 * group[0] + at] = each

    for own in (True, False):
        for at in range(0, rows // 2, GROUP):
            run(own, list(range(at, at + GROUP)))

    half = rows
    deep = tile_ref.shape[1]
    tile_ref[:, :half, :] = first_ref[:, pl.ds(other_rows * half, half), :]

    def partials(at, others):
        left = left_ref[at].reshape(total // 8, 8, width)
        return [
            jnp.sum(left * right_ref[other].reshape(total // 8, 8, width), axis=0)
            for other in others
        ]

    for at in range(0, rows, 2):
        for each in (at, at + 1):
            tri_ref[each, :8, :] = sum_down(partials(each, range(8)))
        both = sum_down(partials(at, range(8, half)) + partials(at + 1, range(8, half)))
        tri_ref[at, 8:half, :] = both[: half - 8]
        tri_ref[at + 1, 8:half, :] = both[half - 8 :]
    first = tile_ref[...].reshape(rows * deep, width)
    tri = tri_ref[...].reshape(rows * deep, width)
    mixed = norm(first).astype(BF16)
    gate = jax.nn.sigmoid(dot(mixed, mult_gate_ref[...]))
    second = first + gate * dot(norm(tri).astype(BF16), mult_out_ref[...])
    hidden = jax.nn.relu(dot(norm(second).astype(BF16), trans_up_ref[...])).astype(BF16)
    result = second + dot(hidden, trans_down_ref[...])
    result_ref[...] = result.astype(BF16).reshape(rows, deep, width)[:, :half, :]


def gathered(
    pair,
    length,
    chain,
    att_proj,
    att_bias,
    chain_bias,
    att_out,
    mult_in,
    mult_gate,
    mult_out,
    trans_up,
    trans_down,
):
    rows, cols, width = pair.shape
    row_count = lax.axis_size("row")
    col_count = lax.axis_size("col")
    sub_count = lax.axis_size("sub")
    total = rows * row_count
    heads = att_bias.shape[1] * sub_count
    axes = ("row", "col", "sub")
    side = 2 * WIDE

    def place(row, col, sub):
        return (row * col_count + col) * sub_count + sub

    def ahead(row, step):
        return row ^ step if FLIP else (row + step) % row_count

    def exchange(value, offsets):
        routes = [
            (place(row, col, sub), place(ahead(row, offsets[sub][0]), col ^ offsets[sub][1], sub))
            for row in range(row_count)
            for col in range(col_count)
            for sub in range(sub_count)
        ]
        return lax.ppermute(value, axes, routes)

    swap = functools.partial(lax.ppermute, axis_name="sub", perm=[(0, 1), (1, 0)])
    fetched = []
    for offsets in STEPS:
        fetched.append(exchange(pair, offsets))
    proj_other = swap(att_proj)
    out_other = swap(att_out)
    bias_other = swap(att_bias)
    chain_other = swap(chain_bias)
    blocks, sources = [], []
    for value, offsets in zip(fetched, STEPS):
        if offsets == ((0, 1), (0, 1)):
            near = value
            continue
        mine = tuple(zip(offsets[0], offsets[1]))
        blocks.append(value)
        sources.append(mine)
        if offsets[0] != offsets[1]:
            blocks.append(swap(value))
            sources.append(tuple((b, a) for a, b in mine))
    vmem = pl.BlockSpec(memory_space=pltpu.VMEM)
    hbm = pl.BlockSpec(memory_space=pltpu.HBM)
    params = [
        chain.reshape(1, total),
        pair,
        att_proj.transpose(1, 2, 0),
        att_bias.T,
        chain_bias.reshape(1, -1),
        att_out,
        mult_in,
        mult_gate,
        mult_out,
        trans_up,
        trans_down,
    ]
    params = [pltpu.with_memory_space_constraint(each, pltpu.HBM) for each in params]
    early = [
        near,
        proj_other.transpose(1, 2, 0),
        bias_other.T,
        chain_other.reshape(1, -1),
        out_other,
    ]
    shape = jax.ShapeDtypeStruct
    scratch = lambda each: pltpu.VMEM(each.shape, each.dtype)
    ready = pl.pallas_call(
        prepare,
        out_shape=[
            shape((3 * width, width), BF16),
            shape((width, width), BF16),
            shape((width, width), BF16),
            shape((8, width), F32),
            shape((heads, total, side), F32),
            shape((total, width), F32),
            shape((rows, WIDE, width), F32),
            shape((rows, WIDE, width), F32),
            shape((rows // 2, heads * total, side), F32),
            shape((rows // 2, width, side), BF16),
            shape((rows // 2, width, side), F32),
            shape((rows, 8, side), F32),
            *[shape(each.shape, each.dtype) for each in params[-5:]],
        ],
        in_specs=[pl.BlockSpec(memory_space=pl.ANY)] + [hbm] * len(params) + [vmem] * len(early),
        out_specs=[vmem] * 17,
        scratch_shapes=[
            scratch(params[0]),
            scratch(params[1]),
            scratch(params[2]),
            scratch(params[3]),
            scratch(params[4]),
            scratch(params[5]),
            pltpu.SMEM((1,), jnp.int32),
            pltpu.SemaphoreType.DMA((len(params) + 1,)),
        ],
        compiler_params=pltpu.CompilerParams(vmem_limit_bytes=LIMIT),
    )(length, *params, *early)
    last = sources[-1][0]
    others = [[step for step in range(1, row_count) if step != late] for late in last]
    merged = pl.pallas_call(
        functools.partial(
            collect, sources=tuple(sources[:-1]), row_steps=tuple(zip(*others)), late_step=last
        ),
        out_shape=[shape((total, 8, side), F32)] + [shape((rows, WIDE, width), F32)] * 3,
        in_specs=[vmem] * (len(blocks) + 3),
        out_specs=[vmem] * 4,
        scratch_shapes=[pltpu.VMEM((total, WIDE, width), F32)] * 2,
        compiler_params=pltpu.CompilerParams(vmem_limit_bytes=LIMIT),
    )(*blocks[:-1], ready[3], ready[6], ready[7], ready[11])
    operands = [blocks[-1], *ready, *merged]
    deep = 16
    return pl.pallas_call(
        functools.partial(finish, source=sources[-1]),
        out_shape=shape((rows, cols // sub_count, width), BF16),
        in_specs=[vmem] * len(operands),
        out_specs=vmem,
        scratch_shapes=[
            *[pltpu.VMEM((2 * rows, WIDE, width), F32)] * 2,
            pltpu.VMEM((rows, WIDE, width), F32),
            pltpu.VMEM((total, 8, side), F32),
            pltpu.VMEM((heads * total, side), F32),
            pltpu.VMEM((rows, total, width), F32),
            pltpu.VMEM((rows, total, width), F32),
            pltpu.VMEM((rows, total, width), F32),
            pltpu.VMEM((rows, deep, width), F32),
            pltpu.VMEM((rows, deep, width), F32),
        ],
        compiler_params=pltpu.CompilerParams(vmem_limit_bytes=LIMIT),
    )(*operands)


def solution(mesh):
    placed = (
        P(("grp", "row"), "col", None),
        P("grp"),
        P("grp"),
        P(None, None, "sub"),
        P(None, "sub"),
        P("sub"),
        P("sub", None),
        P(),
        P(),
        P(),
        P(),
        P(),
    )
    fits = replicated(mesh)
    return jax.shard_map(
        gathered if fits else local,
        mesh=mesh,
        in_specs=placed,
        out_specs=P(("grp", "row"), ("col", "sub"), None),
        check_vma=False,
    )
```

```python
import functools

import jax
import jax.numpy as jnp
from jax import lax
from jax.experimental import pallas as pl
from jax.experimental.pallas import tpu as pltpu
from jax.sharding import PartitionSpec as P


def norm(value):
    mean = jnp.mean(value, axis=-1, keepdims=True)
    centred = value - mean
    variance = jnp.mean(centred * centred, axis=-1, keepdims=True)
    return centred * lax.rsqrt(variance + 1e-05)


def local(
    pair,
    length,
    chain,
    att_proj,
    att_bias,
    chain_bias,
    att_out,
    mult_in,
    mult_gate,
    mult_out,
    trans_up,
    trans_down,
):
    rows, cols, width = pair.shape
    row_count = lax.axis_size("row")
    sub_count = lax.axis_size("sub")
    row_index = lax.axis_index("row")
    col_index = lax.axis_index("col")
    sub_index = lax.axis_index("sub")
    total = rows * row_count
    half = cols // sub_count
    heads_here = att_bias.shape[1]
    spread = att_out.shape[0]
    head_dim = spread // heads_here
    mult_width = mult_out.shape[0]
    valid = (jnp.arange(total) < length[0]).astype(jnp.float32)
    normed = norm(pair.astype(jnp.float32)).astype(jnp.bfloat16)
    flat = normed.reshape(rows * cols, width)
    projected = jnp.dot(
        flat, att_proj.reshape(width, 4 * spread), preferred_element_type=jnp.float32
    ).reshape(rows, cols, 4, spread)
    query = (projected[:, :, 0] * head_dim ** (-0.5)).astype(jnp.bfloat16)
    keys = projected[:, :, 1].astype(jnp.bfloat16)
    values = projected[:, :, 2].astype(jnp.bfloat16)
    gating = jax.nn.sigmoid(projected[:, :, 3])
    bias_local = (
        jnp.dot(flat, att_bias, preferred_element_type=jnp.float32)
        .reshape(rows, cols, heads_here)
        .transpose(2, 0, 1)
    )
    keys_all, values_all = (
        lax.all_gather(keys, "col", axis=1, tiled=True),
        lax.all_gather(values, "col", axis=1, tiled=True),
    )
    column_bias = lax.all_gather(bias_local, "row", axis=1, tiled=True)
    bias_here = lax.all_to_all(column_bias, "col", split_axis=1, concat_axis=2, tiled=True)
    chain_here = lax.dynamic_slice_in_dim(chain, col_index * cols, cols, 0)
    same = (chain_here[:, None] == chain[None, :]).astype(jnp.float32)
    bias_here = (
        bias_here
        + chain_bias[:, None, None] * same[None]
        + (valid[None, None, :] - 1.0) * 1000000000.0
    )

    def attend(block):
        block_query, block_keys, block_values = block
        scores = (
            jnp.einsum(
                "ajhd,akhd->ahjk", block_query, block_keys, preferred_element_type=jnp.float32
            )
            + bias_here[None]
        )
        weights = jax.nn.softmax(scores, axis=-1).astype(jnp.bfloat16)
        return jnp.einsum(
            "ahjk,akhd->ajhd", weights, block_values, preferred_element_type=jnp.float32
        )

    attended = lax.map(
        attend,
        (
            query.reshape(rows // 2, 2, cols, heads_here, head_dim),
            keys_all.reshape(rows // 2, 2, total, heads_here, head_dim),
            values_all.reshape(rows // 2, 2, total, heads_here, head_dim),
        ),
    )
    attended = (attended.reshape(rows, cols, spread) * gating).astype(jnp.bfloat16)
    update = jnp.dot(
        attended.reshape(rows * cols, spread), att_out, preferred_element_type=jnp.float32
    ).reshape(rows, cols, width)
    update_half = lax.psum_scatter(
        update.astype(jnp.bfloat16), "sub", scatter_dimension=1, tiled=True
    ).astype(jnp.float32)
    pair_half = lax.dynamic_slice_in_dim(pair, sub_index * half, half, 1).astype(jnp.float32)
    first = pair_half + update_half
    mixed = norm(first).astype(jnp.bfloat16)
    mixed_flat = mixed.reshape(rows * half, width)
    quad = jnp.dot(mixed_flat, mult_in, preferred_element_type=jnp.float32).reshape(
        rows, half, 4, mult_width
    )
    row_valid = lax.dynamic_slice_in_dim(valid, row_index * rows, rows, 0)
    col_valid = lax.dynamic_slice_in_dim(valid, col_index * cols + sub_index * half, half, 0)
    outer = row_valid[:, None, None] * col_valid[None, :, None]
    left = (outer * jax.nn.sigmoid(quad[:, :, 1]) * quad[:, :, 0]).astype(jnp.bfloat16)
    right = (outer * jax.nn.sigmoid(quad[:, :, 3]) * quad[:, :, 2]).astype(jnp.bfloat16)
    gate_out = jax.nn.sigmoid(jnp.dot(mixed_flat, mult_gate, preferred_element_type=jnp.float32))
    partial_value = jnp.einsum(
        "ikc,jkc->ijc",
        left,
        lax.all_gather(right, "row", axis=0, tiled=True),
        preferred_element_type=jnp.float32,
    )
    tri = lax.psum_scatter(
        partial_value.astype(jnp.bfloat16), ("col", "sub"), scatter_dimension=1, tiled=True
    ).astype(jnp.float32)
    tri_normed = norm(tri).astype(jnp.bfloat16).reshape(rows * half, mult_width)
    second = first + (
        gate_out * jnp.dot(tri_normed, mult_out, preferred_element_type=jnp.float32)
    ).reshape(rows, half, width)
    last_normed = norm(second).astype(jnp.bfloat16).reshape(rows * half, width)
    hidden = jax.nn.relu(jnp.dot(last_normed, trans_up, preferred_element_type=jnp.float32)).astype(
        jnp.bfloat16
    )
    result = second + jnp.dot(hidden, trans_down, preferred_element_type=jnp.float32).reshape(
        rows, half, width
    )
    return result.astype(jnp.bfloat16)


NT = (((1,), (1,)), ((), ()))
TN = (((0,), (0,)), ((), ()))
F32 = jnp.float32
BF16 = jnp.bfloat16
WIDE = 64
FLIP = False
GROUP = 6
LIMIT = 16 * 1024 * 1024
STEPS = (((1, 0), (2, 1)), ((3, 0), (3, 1)), ((0, 1), (0, 1)), ((2, 0), (1, 1)))


def moved(row, step, count, sign):
    return row ^ step if FLIP else lax.rem(row + count + sign * step, count)


def replicated(mesh):
    shape = mesh.shape
    return shape["row"] == 4 and shape["col"] == 2 and shape["sub"] == 2


def dot(left, right, dims=(((1,), (0,)), ((), ()))):
    return lax.dot_general(left, right, dims, preferred_element_type=F32)


def flat_pair(ref, start):
    both = ref[pl.ds(start, 2)].astype(BF16)
    pad = jnp.zeros((WIDE - both.shape[1], both.shape[2]), BF16)
    return jnp.concatenate([both[0], pad, both[1], pad], axis=0)


def head_masks(heads, width):
    channel = lax.broadcasted_iota(jnp.int32, (1, width), 1)
    size = width // heads
    return [
        ((channel >= head * size) & (channel < (head + 1) * size)).astype(BF16)
        for head in range(heads)
    ]


def lane_masks():
    lane = lax.broadcasted_iota(jnp.int32, (1, 2 * WIDE), 1)
    return (lane < WIDE).astype(BF16), (lane >= WIDE).astype(BF16)


def project(tokens, turned_weights, key_weights, heads, total):
    width = tokens[0].shape[1]
    first_lanes, second_lanes = lane_masks()
    masks = head_masks(heads, width)
    turned = [dot(turned_weights, flat, NT) for flat in tokens]
    keys = [dot(flat, key_weights, NT).astype(BF16) for flat in tokens]
    scores = []
    for key, turn in zip(keys, turned):
        query = (turn[:width] * (width // heads) ** (-0.5)).astype(BF16)
        spread_keys = jnp.concatenate(
            [
                jnp.concatenate([key[at : at + total] * mask for mask in masks], axis=0)
                for at in (0, WIDE)
            ],
            axis=1,
        )
        spread_query = jnp.concatenate([query * first_lanes, query * second_lanes], axis=0)
        scores.append(dot(spread_keys, spread_query))
    values = [turn[width : 2 * width].astype(BF16) for turn in turned]
    gates = [jax.nn.sigmoid(turn[2 * width :]) for turn in turned]
    return scores, values, gates


def block_norm(ref):
    block = ref[...]
    flat = block.reshape(-1, block.shape[-1])
    ones = jnp.full((block.shape[-1], block.shape[-1]), 1.0 / block.shape[-1], BF16)
    value = flat.astype(F32)
    centred = value - dot(flat, ones)
    variance = jnp.mean(centred * centred, axis=-1, keepdims=True)
    result = centred * lax.rsqrt(variance + 1e-05)
    return value.reshape(block.shape), result.reshape(block.shape)


def split_norm(value):
    width = value.shape[-1]
    high = value.astype(BF16)
    low = (value - high.astype(F32)).astype(BF16)
    ones = jnp.full((2 * width, width), 1.0 / width, BF16)
    centred = value - dot(jnp.concatenate([high, low], axis=1), ones)
    variance = jnp.mean(centred * centred, axis=-1, keepdims=True)
    return centred * lax.rsqrt(variance + 1e-05)


def sum_down(parts):
    row = lax.broadcasted_iota(jnp.int32, parts[0].shape, 0)
    for distance in (1, 2, 4):
        keep = (row & distance) == 0
        parts = [
            jnp.where(keep, one, two) + pltpu.roll(jnp.where(keep, two, one), distance, 0)
            for one, two in zip(parts[0::2], parts[1::2])
        ]
    return parts[0]


def bias_rows(weights, tokens, turn_ref, row):
    both = dot(weights, tokens, NT)
    turn_ref[row] = both
    turn_ref[row + 1] = pltpu.roll(both, WIDE, 1)


def prepare(
    length_any,
    chain_hbm,
    own_hbm,
    proj_hbm,
    att_bias_hbm,
    chain_bias_hbm,
    out_hbm,
    mult_in_hbm,
    mult_gate_hbm,
    mult_out_hbm,
    trans_up_hbm,
    trans_down_hbm,
    near_ref,
    proj_other_ref,
    att_bias_other_ref,
    chain_bias_other_ref,
    out_other_ref,
    turned_weights_ref,
    key_weights_ref,
    out_weights_ref,
    att_bias_ref,
    plain_bias_ref,
    valid_ref,
    raw_ref,
    normed_ref,
    scores_ref,
    values_ref,
    gates_ref,
    turn_ref,
    mult_in_ref,
    mult_gate_ref,
    mult_out_ref,
    trans_up_ref,
    trans_down_ref,
    chain_ref,
    own_ref,
    proj_ref,
    att_bias_own_ref,
    chain_bias_ref,
    out_ref,
    length_ref,
    copy_sems,
):
    pairs = (
        (own_hbm, own_ref),
        (proj_hbm, proj_ref),
        (chain_hbm, chain_ref),
        (att_bias_hbm, att_bias_own_ref),
        (chain_bias_hbm, chain_bias_ref),
        (out_hbm, out_ref),
        (length_any, length_ref),
        (mult_in_hbm, mult_in_ref),
        (mult_gate_hbm, mult_gate_ref),
        (mult_out_hbm, mult_out_ref),
        (trans_up_hbm, trans_up_ref),
        (trans_down_hbm, trans_down_ref),
    )
    copies = [
        pltpu.make_async_copy(src, dst, copy_sems.at[at]) for at, (src, dst) in enumerate(pairs)
    ]
    for copy in copies:
        copy.start()
    rows, cols, width = own_ref.shape
    heads = plain_bias_ref.shape[0]
    total = plain_bias_ref.shape[1]
    col_index = lax.axis_index("col")
    att_bias_ref[...] = jnp.zeros(att_bias_ref.shape, F32)
    for ref, col in ((near_ref, 1 - col_index), (own_ref, col_index)):
        if ref is own_ref:
            for copy in copies[:7]:
                copy.wait()
        at = pl.ds(pl.multiple_of(col * cols, 8), cols)
        value, result = block_norm(ref)
        raw_ref[:, at, :] = value
        normed_ref[:, at, :] = result
    for part, at in ((1, None), (0, 0), (2, 1), (3, 2)):
        both = jnp.concatenate([proj_ref[part], proj_other_ref[part]], axis=0)
        if at is None:
            key_weights_ref[...] = both
        else:
            turned_weights_ref[at * width : (at + 1) * width] = both
    out_weights_ref[...] = jnp.concatenate([out_ref[...], out_other_ref[...]], axis=0)
    att_bias_ref[0 : heads // 2] = att_bias_own_ref[...].astype(F32)
    att_bias_ref[heads // 2 : heads] = att_bias_other_ref[...].astype(F32)
    length = length_ref[0]
    side = 2 * WIDE
    chain = chain_ref[...].astype(F32)
    chain = jnp.concatenate([chain, jnp.zeros((1, side - total), F32)], axis=1)
    chain = jnp.broadcast_to(chain, (side, side))
    same = (chain == chain.T).astype(F32)[:total]
    place = lax.broadcasted_iota(jnp.int32, (total, side), 1)
    masked = jnp.where(place < length, 0.0, -1000000000.0)
    for head in range(heads):
        from_ref = chain_bias_ref if head < heads // 2 else chain_bias_other_ref
        at = head % (heads // 2)
        plain_bias_ref[head, :, :] = from_ref[:, at : at + 1] * same + masked
    down = lax.broadcasted_iota(jnp.int32, (total, width), 0)
    valid_ref[...] = (down < length).astype(F32)
    tokens = [flat_pair(normed_ref, 2 * at) for at in range(rows // 2)]
    weights = att_bias_ref[...].astype(BF16)
    for at in range(rows // 2):
        bias_rows(weights, tokens[at], turn_ref, 2 * at)
    scores, values, gates = project(
        tokens, turned_weights_ref[...], key_weights_ref[...], heads, total
    )
    for at in range(rows // 2):
        scores_ref[at] = scores[at]
        values_ref[at] = values[at]
        gates_ref[at] = gates[at]
    for copy in copies[7:]:
        copy.wait()


def scatter(block_refs, sources, raw_ref, normed_ref):
    sub_index = lax.axis_index("sub")
    for ref, (row_step, col_step) in zip(block_refs, sources):
        rows, cols, _ = ref.shape
        row_block = moved(
            lax.axis_index("row"), jnp.where(sub_index == 0, *row_step), lax.axis_size("row"), -1
        )
        col_block = lax.axis_index("col") ^ jnp.where(sub_index == 0, *col_step)
        down = pl.ds(row_block * rows, rows)
        along = pl.ds(pl.multiple_of(col_block * cols, 8), cols)
        value, result = block_norm(ref)
        raw_ref[down, along, :] = value
        normed_ref[down, along, :] = result


def whole_rows(att_bias_ref, normed_ref, turn_ref, rows, row_step):
    weights = att_bias_ref[...].astype(BF16)
    start = moved(
        lax.axis_index("row"),
        jnp.where(lax.axis_index("sub") == 0, *row_step),
        lax.axis_size("row"),
        -1,
    )
    start = start * rows
    for at in range(rows // 2):
        tokens = flat_pair(normed_ref, start + 2 * at)
        bias_rows(weights, tokens, turn_ref, start + 2 * at)


def collect(*refs, sources, row_steps, late_step):
    count = len(sources)
    (
        att_bias_ref,
        raw_own_ref,
        normed_own_ref,
        turn_own_ref,
        turn_ref,
        raw_other_ref,
        normed_other_ref,
        normed_late_ref,
        raw_ref,
        normed_ref,
    ) = refs[count:]
    rows = raw_own_ref.shape[0]
    row_index = lax.axis_index("row")
    sub_index = lax.axis_index("sub")
    scatter(refs[:count], sources, raw_ref, normed_ref)
    own_rows = pl.ds(row_index * rows, rows)
    raw_ref[own_rows] = raw_own_ref[...]
    normed_ref[own_rows] = normed_own_ref[...]
    turn_ref[own_rows] = turn_own_ref[...]
    for row_step in row_steps:
        whole_rows(att_bias_ref, normed_ref, turn_ref, rows, row_step)
    other_rows = lax.axis_index("col") * lax.axis_size("sub") + sub_index
    late_rows = moved(
        row_index, jnp.where(sub_index == 0, *late_step), lax.axis_size("row"), -1
    )
    raw_other_ref[...] = raw_ref[pl.ds(other_rows * rows, rows)]
    normed_other_ref[...] = normed_ref[pl.ds(other_rows * rows, rows)]
    normed_late_ref[...] = normed_ref[pl.ds(late_rows * rows, rows)]


def finish(*refs, source):
    (
        block_ref,
        turned_weights_ref,
        key_weights_ref,
        out_weights_ref,
        att_bias_ref,
        plain_bias_ref,
        valid_ref,
        raw_own_ref,
        _,
        scores_ref,
        values_ref,
        gates_ref,
        _,
        mult_in_ref,
        mult_gate_ref,
        mult_out_ref,
        trans_up_ref,
        trans_down_ref,
        turn_early_ref,
        raw_early_ref,
        normed_early_ref,
        late_early_ref,
        result_ref,
        raw_ref,
        normed_ref,
        late_ref,
        turn_ref,
        bias_ref,
        left_ref,
        right_ref,
        first_ref,
        tile_ref,
        tri_ref,
    ) = refs
    rows, cols, width = block_ref.shape
    total = valid_ref.shape[0]
    heads = plain_bias_ref.shape[0]
    head_dim = width // heads
    row_index = lax.axis_index("row")
    col_index = lax.axis_index("col")
    sub_index = lax.axis_index("sub")
    other_rows = col_index * lax.axis_size("sub") + sub_index
    side = 2 * WIDE

    row_step, col_step = source
    late_rows = moved(
        row_index, jnp.where(sub_index == 0, *row_step), lax.axis_size("row"), -1
    )
    col_block = col_index ^ jnp.where(sub_index == 0, *col_step)
    along = pl.ds(pl.multiple_of(col_block * cols, 8), cols)
    value, result = block_norm(block_ref)
    late_ref[...] = late_early_ref[...]
    late_ref[:, along, :] = result
    turn_ref[...] = turn_early_ref[...]
    weights = att_bias_ref[...].astype(BF16)
    for at in range(rows // 2):
        tokens = flat_pair(late_ref, 2 * at)
        bias_rows(weights, tokens, turn_ref, late_rows * rows + 2 * at)
    here = pl.ds(jnp.where(other_rows == late_rows, 0, rows), rows)
    raw_ref[:rows] = raw_early_ref[...]
    normed_ref[:rows] = normed_early_ref[...]
    raw_ref[here, along, :] = value
    normed_ref[here, along, :] = result

    for head in range(heads):
        value = turn_ref[:, head, :] + plain_bias_ref[head]
        value = jnp.concatenate([value, jnp.zeros((WIDE - total, side), F32)], axis=0)
        value = jnp.concatenate([value, value], axis=0).T
        bias_ref[pl.ds(head * total, total)] = value[:total]

    first_lanes, second_lanes = lane_masks()
    pad = jnp.zeros((WIDE - total, side), BF16)
    out_weights = out_weights_ref[...]

    def soften(scores):
        weights = []
        for head in range(heads):
            at = slice(head * total, (head + 1) * total)
            bias = bias_ref[at]
            parts = [score[at] + bias for score in scores]
            parts = [jnp.exp(part - jnp.max(part, axis=0, keepdims=True)) for part in parts]
            weights.append(
                [(part / jnp.sum(part, axis=0, keepdims=True)).astype(BF16) for part in parts]
            )
        return list(zip(*weights))

    def update(raws, weights, values, gates):
        attended = []
        for each, value, gate in zip(weights, values, gates):
            parts = []
            for head in range(heads):
                spread_weights = jnp.concatenate(
                    [each[head] * first_lanes, pad, each[head] * second_lanes, pad], axis=0
                )
                parts.append(dot(value[head * head_dim : (head + 1) * head_dim], spread_weights))
            attended.append((jnp.concatenate(parts, axis=0) * gate).astype(BF16))
        updates = [dot(each, out_weights, TN) for each in attended]
        updates = [
            jnp.concatenate([each[:total], each[WIDE : WIDE + total]], axis=0) for each in updates
        ]
        return [raw.reshape(2 * total, width) + each for raw, each in zip(raws, updates)]

    valid = valid_ref[...]

    def side_of(firsts, column):
        mixed = [split_norm(first).astype(BF16) for first in firsts]
        boths = [dot(each, mult_in_ref[:, column : column + 2 * width]) for each in mixed]
        values = [jax.nn.sigmoid(both[:, width:]) * both[:, :width] for both in boths]
        return [value[at : at + total] for value in values for at in (0, total)]

    steps = range(rows // 2)

    def own_first(group, weights):
        return update(
            [raw_own_ref[2 * at : 2 * at + 2] for at in group],
            weights,
            [values_ref[at] for at in group],
            [gates_ref[at] for at in group],
        )

    def own_side(group, firsts):
        for at, first in zip(group, firsts):
            first_ref[2 * at : 2 * at + 2] = first.reshape(2, total, width)
        for at, each in enumerate(side_of(firsts, 0)):
            left_ref[2 * group[0] + at] = each * valid

    def other_first(group, weights):
        return update(
            [raw_ref[2 * at : 2 * at + 2] for at in group],
            weights,
            [values[at] for at in group],
            [gates[at] for at in group],
        )

    def other_side(group, firsts):
        for at, each in enumerate(side_of(firsts, 2 * width)):
            right_ref[2 * group[0] + at] = each

    tokens = [flat_pair(normed_ref, 2 * at) for at in steps]
    scores, values, gates = project(
        tokens, turned_weights_ref[...], key_weights_ref[...], heads, total
    )
    groups = [list(steps)[at : at + GROUP] for at in range(0, len(steps), GROUP)]
    for group in groups:
        other = soften([scores[at] for at in group])
        own = soften([scores_ref[at] for at in group])
        other = other_first(group, other)
        own = own_first(group, own)
        other_side(group, other)
        own_side(group, own)
    half = rows
    deep = tile_ref.shape[1]
    tile_ref[:, :half, :] = first_ref[:, pl.ds(other_rows * half, half), :]

    def partials(at, others):
        left = left_ref[at].reshape(total // 8, 8, width)
        return [
            jnp.sum(left * right_ref[other].reshape(total // 8, 8, width), axis=0)
            for other in others
        ]

    for at in range(0, rows, 2):
        for each in (at, at + 1):
            tri_ref[each, :8, :] = sum_down(partials(each, range(8)))
        both = sum_down(partials(at, range(8, half)) + partials(at + 1, range(8, half)))
        tri_ref[at, 8:half, :] = both[: half - 8]
        tri_ref[at + 1, 8:half, :] = both[half - 8 :]
    first = tile_ref[...].reshape(rows * deep, width)
    row_valid = valid_ref[pl.ds(row_index * rows, rows), :].reshape(rows, 1, width)
    other_valid = valid_ref[pl.ds(other_rows * half, half), :].reshape(1, half, width)
    tri_ref[:, :half, :] = tri_ref[:, :half, :] * (row_valid * other_valid)
    tri = tri_ref[...].reshape(rows * deep, width)
    mixed = norm(first).astype(BF16)
    gate = jax.nn.sigmoid(dot(mixed, mult_gate_ref[...]))
    second = first + gate * dot(norm(tri).astype(BF16), mult_out_ref[...])
    hidden = jax.nn.relu(dot(norm(second).astype(BF16), trans_up_ref[...])).astype(BF16)
    result = second + dot(hidden, trans_down_ref[...])
    result_ref[...] = result.astype(BF16).reshape(rows, deep, width)[:, :half, :]


def gathered(
    pair,
    length,
    chain,
    att_proj,
    att_bias,
    chain_bias,
    att_out,
    mult_in,
    mult_gate,
    mult_out,
    trans_up,
    trans_down,
):
    rows, cols, width = pair.shape
    row_count = lax.axis_size("row")
    col_count = lax.axis_size("col")
    sub_count = lax.axis_size("sub")
    total = rows * row_count
    heads = att_bias.shape[1] * sub_count
    axes = ("row", "col", "sub")
    side = 2 * WIDE

    def place(row, col, sub):
        return (row * col_count + col) * sub_count + sub

    def ahead(row, step):
        return row ^ step if FLIP else (row + step) % row_count

    def exchange(value, offsets):
        routes = [
            (place(row, col, sub), place(ahead(row, offsets[sub][0]), col ^ offsets[sub][1], sub))
            for row in range(row_count)
            for col in range(col_count)
            for sub in range(sub_count)
        ]
        return lax.ppermute(value, axes, routes)

    swap = functools.partial(lax.ppermute, axis_name="sub", perm=[(0, 1), (1, 0)])
    fetched = []
    for offsets in STEPS:
        fetched.append(exchange(pair, offsets))
    proj_other = swap(att_proj)
    out_other = swap(att_out)
    bias_other = swap(att_bias)
    chain_other = swap(chain_bias)
    blocks, sources = [], []
    for value, offsets in zip(fetched, STEPS):
        if offsets == ((0, 1), (0, 1)):
            near = value
            continue
        mine = tuple(zip(offsets[0], offsets[1]))
        blocks.append(value)
        sources.append(mine)
        if offsets[0] != offsets[1]:
            blocks.append(swap(value))
            sources.append(tuple((b, a) for a, b in mine))
    vmem = pl.BlockSpec(memory_space=pltpu.VMEM)
    hbm = pl.BlockSpec(memory_space=pltpu.HBM)
    params = [
        chain.reshape(1, total),
        pair,
        att_proj.transpose(1, 2, 0),
        att_bias.T,
        chain_bias.reshape(1, -1),
        att_out,
        mult_in,
        mult_gate,
        mult_out,
        trans_up,
        trans_down,
    ]
    params = [pltpu.with_memory_space_constraint(each, pltpu.HBM) for each in params]
    early = [
        near,
        proj_other.transpose(1, 2, 0),
        bias_other.T,
        chain_other.reshape(1, -1),
        out_other,
    ]
    shape = jax.ShapeDtypeStruct
    scratch = lambda each: pltpu.VMEM(each.shape, each.dtype)
    ready = pl.pallas_call(
        prepare,
        out_shape=[
            shape((3 * width, width), BF16),
            shape((width, width), BF16),
            shape((width, width), BF16),
            shape((8, width), F32),
            shape((heads, total, side), F32),
            shape((total, width), F32),
            shape((rows, total, width), F32),
            shape((rows, total, width), F32),
            shape((rows // 2, heads * total, side), F32),
            shape((rows // 2, width, side), BF16),
            shape((rows // 2, width, side), F32),
            shape((rows, 8, side), F32),
            *[shape(each.shape, each.dtype) for each in params[-5:]],
        ],
        in_specs=[pl.BlockSpec(memory_space=pl.ANY)] + [hbm] * len(params) + [vmem] * len(early),
        out_specs=[vmem] * 17,
        scratch_shapes=[
            scratch(params[0]),
            scratch(params[1]),
            scratch(params[2]),
            scratch(params[3]),
            scratch(params[4]),
            scratch(params[5]),
            pltpu.SMEM((1,), jnp.int32),
            pltpu.SemaphoreType.DMA((len(params) + 1,)),
        ],
        compiler_params=pltpu.CompilerParams(vmem_limit_bytes=LIMIT),
    )(length, *params, *early)
    last = sources[-1][0]
    others = [[step for step in range(1, row_count) if step != late] for late in last]
    merged = pl.pallas_call(
        functools.partial(
            collect, sources=tuple(sources[:-1]), row_steps=tuple(zip(*others)), late_step=last
        ),
        out_shape=[shape((total, 8, side), F32)] + [shape((rows, total, width), F32)] * 3,
        in_specs=[vmem] * (len(blocks) + 3),
        out_specs=[vmem] * 4,
        scratch_shapes=[pltpu.VMEM((total, total, width), F32)] * 2,
        compiler_params=pltpu.CompilerParams(vmem_limit_bytes=LIMIT),
    )(*blocks[:-1], ready[3], ready[6], ready[7], ready[11])
    operands = [blocks[-1], *ready, *merged]
    deep = 16
    return pl.pallas_call(
        functools.partial(finish, source=sources[-1]),
        out_shape=shape((rows, cols // sub_count, width), BF16),
        in_specs=[vmem] * len(operands),
        out_specs=vmem,
        scratch_shapes=[
            *[pltpu.VMEM((2 * rows, total, width), F32)] * 2,
            pltpu.VMEM((rows, total, width), F32),
            pltpu.VMEM((total, 8, side), F32),
            pltpu.VMEM((heads * total, side), F32),
            pltpu.VMEM((rows, total, width), F32),
            pltpu.VMEM((rows, total, width), F32),
            pltpu.VMEM((rows, total, width), F32),
            pltpu.VMEM((rows, deep, width), F32),
            pltpu.VMEM((rows, deep, width), F32),
        ],
        compiler_params=pltpu.CompilerParams(vmem_limit_bytes=LIMIT),
    )(*operands)


def solution(mesh):
    placed = (
        P(("grp", "row"), "col", None),
        P("grp"),
        P("grp"),
        P(None, None, "sub"),
        P(None, "sub"),
        P("sub"),
        P("sub", None),
        P(),
        P(),
        P(),
        P(),
        P(),
    )
    fits = replicated(mesh)
    return jax.shard_map(
        gathered if fits else local,
        mesh=mesh,
        in_specs=placed,
        out_specs=P(("grp", "row"), ("col", "sub"), None),
        check_vma=False,
    )
```
